512 devices in a mesh: seq: 32 (over z, core), head: 16 (over y, x).
Axes of the slice: x: 4, y: 4, z: 16, core: 2. Of those that a mesh axis runs over, the one named last changes fastest.
Arguments:
- queries: bfloat16 [4096, 8192], P('seq', 'head'), may hold values from -6 to 6
- key_value: bfloat16 [4096, 2048], P('seq', 'head'), may hold values from -6 to 6
- grad_out: bfloat16 [4096, 8192], P('seq', 'head'), may hold values from -60 to 60
- ssm_grad: bfloat16 [4096, 8192], P('seq', 'head'), may hold values from -60 to 60
- b_proj: bfloat16 [4096, 128], P('seq'), may hold values from -1.5 to 1.5
- c_proj: bfloat16 [4096, 128], P('seq'), may hold values from -1.5 to 1.5
- decay_log: float32 [128, 4096], P('head', 'seq'), may hold values from -1.2 to 0
- skip_gain: float32 [128], P('head'), may hold values from 1 to 16
Outputs:
- grad_queries: bfloat16 [4096, 8192], P('seq', 'head')
- grad_key_value: bfloat16 [4096, 2048], P('seq', 'head')
- grad_ssm_in: bfloat16 [4096, 8192], P('seq', 'head')
The draws below stay inside these ranges and needn't reach their ends.
All inputs are finite; a program needn't handle non-finite values. Where the reference program divides by a largest or mean magnitude, that divisor is 1e-20 or more.
Results may differ from the reference program's by a relative error of at most 0.012.
Values may be sent and summed in bfloat16 or wider, within the bound.
No kernel may reach another device: no remote copies, remote signals or barrier semaphores. Data moves between devices by JAX's collectives and lax.ppermute only.
A program may use at most 64 MiB of HBM per device.

```python
import math
import jax
import jax.numpy as jnp
from jax import lax

HEAD_DIM = 128
Q_HEADS = 64
KV_HEADS = 8
TOK_DEV = 128
SEQUENCE_LENGTH = 4096
SSM_HEADS = 128
SSM_DIM = 64
STATE = 128


def attention_pair(key):
    query_key = jax.random.fold_in(key, 101)
    pair_key = jax.random.fold_in(key, 102)
    group = Q_HEADS // KV_HEADS
    queries = jnp.clip(jax.random.normal(query_key, (SEQUENCE_LENGTH, Q_HEADS, HEAD_DIM), jnp.float32), -6.0, 6.0)
    pairs = jnp.clip(jax.random.normal(pair_key, (SEQUENCE_LENGTH, KV_HEADS, 2, HEAD_DIM), jnp.float32), -6.0, 6.0)
    half_length = SEQUENCE_LENGTH // 2
    earlier_keys = jnp.concatenate([jnp.zeros((SEQUENCE_LENGTH - half_length, KV_HEADS, HEAD_DIM), jnp.float32), pairs[:half_length, :, 0]], axis=0)
    earlier_heads = jnp.repeat(earlier_keys, group, axis=1)
    head_number = jnp.arange(Q_HEADS) % group
    chosen_heads = (head_number == 1) | (head_number == 2)
    late_rows = jnp.arange(SEQUENCE_LENGTH) >= SEQUENCE_LENGTH - half_length
    aligned_mask = late_rows[:, None] & chosen_heads[None, :]
    aligned = jnp.clip(0.8 * earlier_heads + 0.6 * queries, -6.0, 6.0)
    queries = jnp.where(aligned_mask[:, :, None], aligned, queries)
    return (queries.reshape(SEQUENCE_LENGTH, Q_HEADS * HEAD_DIM), pairs.reshape(SEQUENCE_LENGTH, KV_HEADS * 2 * HEAD_DIM))


def draw_queries(key, part):
    return attention_pair(key)[0].astype(jnp.bfloat16)


def draw_key_value(key, part):
    return attention_pair(key)[1].astype(jnp.bfloat16)


def cotangent(key, salt, width):
    base = jax.random.fold_in(key, salt)
    noise_key = jax.random.fold_in(base, 1)
    column_key = jax.random.fold_in(base, 2)
    rising = 0.5 * 10.0 ** (jnp.arange(SEQUENCE_LENGTH, dtype=jnp.float32) / SEQUENCE_LENGTH)
    column = jnp.exp(jax.random.uniform(column_key, (width,), jnp.float32, math.log(0.3), math.log(3.0)))
    noise = jnp.clip(jax.random.normal(noise_key, (SEQUENCE_LENGTH, width), jnp.float32), -4.0, 4.0)
    return noise * rising[:, None] * column[None, :]


def draw_grad_out(key, part):
    return cotangent(key, 201, Q_HEADS * HEAD_DIM).astype(jnp.bfloat16)


def draw_ssm_grad(key, part):
    return cotangent(key, 202, SSM_HEADS * SSM_DIM).astype(jnp.bfloat16)


def draw_decay_log(key, part):
    divide_prng_seeds = [jax.random.fold_in(key, 300 + number) for number in range(7)]
    slow_share = 0.5
    is_slow = jax.random.uniform(divide_prng_seeds[0], (SSM_HEADS,), jnp.float32) < slow_share
    slow_rate = jnp.exp(jax.random.uniform(divide_prng_seeds[1], (SSM_HEADS,), jnp.float32, math.log(0.05 / SEQUENCE_LENGTH), math.log(0.3 / SEQUENCE_LENGTH)))
    fast_rate = jnp.exp(jax.random.uniform(divide_prng_seeds[2], (SSM_HEADS,), jnp.float32, math.log(1.0 / 50.0), math.log(1.0 / 30.0)))
    rate = jnp.where(is_slow, slow_rate, fast_rate)
    shard_factor = jnp.exp(jax.random.uniform(divide_prng_seeds[3], (SSM_HEADS, SEQUENCE_LENGTH // TOK_DEV), jnp.float32, math.log(0.5), math.log(2.0)))
    shard_factor = jnp.repeat(shard_factor, TOK_DEV, axis=1)
    rough = jax.random.uniform(divide_prng_seeds[4], (SSM_HEADS, SEQUENCE_LENGTH), jnp.float32, 0.6, 1.6)
    spike_offset = jax.random.randint(divide_prng_seeds[5], (2,), 0, SEQUENCE_LENGTH)
    keeping = jax.random.uniform(divide_prng_seeds[6], (SSM_HEADS, 2), jnp.float32, 0.6, 0.8)
    agreeing_total = (jnp.arange(SEQUENCE_LENGTH)[None, :] == spike_offset[:, None]).astype(jnp.float32)
    return -rate[:, None] * shard_factor * rough + jnp.dot(jnp.log(keeping), agreeing_total)


def shard_levels(rng, shape, pieces, smallest, largest):
    def one(axis_at, shards_of):
        draws = jax.random.uniform(jax.random.fold_in(jax.random.fold_in(rng, 6), axis_at), (shards_of,), jnp.float32, smallest / len(pieces), largest / len(pieces))
        return jnp.repeat(jnp.exp(draws), shape[axis_at] // shards_of).reshape((-1,) + (1,) * (len(shape) - axis_at - 1))

    gain = one(*pieces[0])
    for cut in pieces[1:]:
        gain = gain * one(*cut)
    return gain


def bell_draw(own_key, shape, scale, limit, cuts=(), held_as=jnp.bfloat16):
    factor_of = shard_levels(own_key, shape, cuts, -0.22, 0.18) if cuts else 1.0
    drawn = jax.random.normal(own_key, shape, jnp.float32) * scale * factor_of
    return jnp.minimum(jnp.maximum(drawn, -limit), limit).astype(held_as)


def setup_inputs(seed: int = 0) -> dict:
    arg_keys = jax.random.split(jax.random.key(seed), 9)
    return {
        "queries": draw_queries(jax.random.fold_in(arg_keys[8], 71), 0),
        "key_value": draw_key_value(jax.random.fold_in(arg_keys[8], 71), 0),
        "grad_out": draw_grad_out(jax.random.fold_in(arg_keys[8], 71), 0),
        "ssm_grad": draw_ssm_grad(jax.random.fold_in(arg_keys[8], 71), 0),
        "b_proj": bell_draw(arg_keys[4], (SEQUENCE_LENGTH, STATE), 0.25, 1.5, ((0, 32),)),
        "c_proj": bell_draw(arg_keys[5], (SEQUENCE_LENGTH, STATE), 0.25, 1.5, ((0, 32),)),
        "decay_log": draw_decay_log(jax.random.fold_in(arg_keys[8], 71), 0),
        "skip_gain": jnp.clip(jnp.exp(math.log(16.0) - 2.7725887 * jax.random.uniform(arg_keys[7], (SSM_HEADS,), jnp.float32) ** shard_levels(arg_keys[7], (SSM_HEADS,), ((0, 16),), -0.2, 0.2)), 1.0, 16.0),
    }


epsilon = 1e-06

def head_backward(items):
    query, grad_head, keys, values = items
    score_scale = 1.0 / math.sqrt(HEAD_DIM)
    positions = jnp.arange(SEQUENCE_LENGTH)
    causal = positions[:, None] >= positions[None, :]
    scores = jnp.dot(query, keys.T, preferred_element_type=jnp.float32) * score_scale
    scores = jnp.where(causal, scores, -jnp.inf)
    peak = lax.optimization_barrier(jnp.max(scores, axis=1, keepdims=True))
    log_total = peak + jnp.log(lax.optimization_barrier(jnp.sum(jnp.exp(scores - peak), axis=1, keepdims=True)))
    probs = jnp.exp(scores - log_total)
    probs_b = probs.astype(jnp.bfloat16)
    out_b = jnp.dot(probs_b, values, preferred_element_type=jnp.float32).astype(jnp.bfloat16)
    out_b = lax.optimization_barrier(out_b)
    delta = lax.optimization_barrier(jnp.sum(grad_head.astype(jnp.float32) * out_b.astype(jnp.float32), axis=1, keepdims=True))
    dprob = jnp.dot(grad_head, values.T, preferred_element_type=jnp.float32)
    dscore_b = (probs * (dprob - delta)).astype(jnp.bfloat16)
    grad_q = jnp.dot(dscore_b, keys, preferred_element_type=jnp.float32) * score_scale
    grad_k = jnp.dot(dscore_b.T, query, preferred_element_type=jnp.float32) * score_scale
    grad_v = jnp.dot(probs_b.T, grad_head, preferred_element_type=jnp.float32)
    return (grad_q, grad_k, grad_v)

def reference(queries, key_value, grad_out, ssm_grad, b_proj, c_proj, decay_log, skip_gain):
    group = Q_HEADS // KV_HEADS
    query_heads = queries.reshape(SEQUENCE_LENGTH, Q_HEADS, HEAD_DIM).transpose(1, 0, 2)
    grad_heads = grad_out.reshape(SEQUENCE_LENGTH, Q_HEADS, HEAD_DIM).transpose(1, 0, 2)
    pairs = key_value.reshape(SEQUENCE_LENGTH, KV_HEADS, 2, HEAD_DIM).transpose(1, 2, 0, 3)
    key_heads = jnp.repeat(pairs[:, 0], group, axis=0)
    value_heads = jnp.repeat(pairs[:, 1], group, axis=0)
    grad_q, grad_k, grad_v = lax.map(head_backward, (query_heads, grad_heads, key_heads, value_heads))
    grad_k = grad_k.reshape(KV_HEADS, group, SEQUENCE_LENGTH, HEAD_DIM).sum(axis=1)
    grad_v = grad_v.reshape(KV_HEADS, group, SEQUENCE_LENGTH, HEAD_DIM).sum(axis=1)
    grad_q = grad_q.transpose(1, 0, 2).reshape(SEQUENCE_LENGTH, Q_HEADS * HEAD_DIM)
    grad_kv = jnp.stack([grad_k, grad_v], axis=1).transpose(2, 0, 1, 3).reshape(SEQUENCE_LENGTH, KV_HEADS * 2 * HEAD_DIM)
    grad_in = ssm_grad.reshape(SEQUENCE_LENGTH, SSM_HEADS, SSM_DIM).astype(jnp.float32)
    decay_next = jnp.concatenate([jnp.exp(decay_log[:, 1:]), jnp.zeros((SSM_HEADS, 1), jnp.float32)], axis=1).T

    def backward_step(state, items):
        grad_row, c_row, b_row, next_decay = items
        state = next_decay[:, None, None] * state + grad_row[:, :, None] * c_row[None, None, :]
        result = jnp.einsum('hpn,n->hp', state, b_row, precision=lax.Precision.HIGHEST)
        return (state, result)
    initial = jnp.zeros((SSM_HEADS, SSM_DIM, STATE), jnp.float32)
    _, grad_x = lax.scan(backward_step, initial, (grad_in, c_proj.astype(jnp.float32), b_proj.astype(jnp.float32), decay_next), reverse=True)
    grad_x = grad_x + skip_gain[None, :, None] * grad_in
    grad_x = grad_x.reshape(SEQUENCE_LENGTH, SSM_HEADS * SSM_DIM)
    scaled_q = (grad_q / (jnp.max(jnp.abs(grad_q)) + epsilon)).astype(jnp.bfloat16)
    scaled_kv = (grad_kv / (jnp.max(jnp.abs(grad_kv)) + epsilon)).astype(jnp.bfloat16)
    scaled_x = (grad_x / (jnp.max(jnp.abs(grad_x)) + epsilon)).astype(jnp.bfloat16)
    return (scaled_q, scaled_kv, scaled_x)
```

```python
import math

import jax
import jax.numpy as jnp
from jax import lax
from jax.experimental import pallas as pl
from jax.experimental.pallas import tpu as pltpu
from jax.sharding import Mesh
from jax.sharding import PartitionSpec as P

SEQ = ("hi", "lo", "c")
HEAD = ("y", "xh", "xp")
SIZES = (4, 4, 2, 4, 2, 2)
CHIPS = 16
TOK = 128
EXTRA = 16
ROWS = TOK + EXTRA
SSM_HEADS = 8
SSM_DIM = 64
SCALE = 1.0 / math.sqrt(128)
EPSILON = 1e-6
HIGHEST = lax.Precision.HIGHEST
f32 = jnp.float32
bf16 = jnp.bfloat16


def dot(a, b, dims, precision=None):
    return lax.dot_general(a, b, (dims, ((), ())), precision=precision, preferred_element_type=f32)


NN = ((1,), (0,))
NT = ((1,), (1,))
TN = ((0,), (0,))


def heads_to_rows(x):
    return jnp.concatenate([x[:, 128 * h : 128 * (h + 1)] for h in range(4)], axis=0)


def attention_kernel(pos_ref, q_ref, do_ref, kv_ref, dq_ref, dkv_ref, peak_ref, s_ref, dp_ref, dqt_ref):
    chip, core = pos_ref[0], pos_ref[1]
    lane_group = lax.rem(chip, 4)
    q = heads_to_rows(q_ref[...])
    do = heads_to_rows(do_ref[...])
    width = q.shape[0]

    def place(z):
        return lax.rem(lax.rem(z, 4) - lane_group + 4, 4), z // 4

    def rows_at(z, c):
        return pl.ds(pl.multiple_of(z * 256 + c * 128, 128), 128)

    def partial_rows(x, op):
        return op(x.reshape(TOK // 8, 8, width), axis=0)

    def score_step(z, peak, masked):
        rel, hi = place(z)
        for c in range(2):
            s = dot(kv_ref[c, rel, hi, 0, :TOK, :], q, NT)
            if masked:
                key = lax.broadcasted_iota(jnp.int32, s.shape, 0) + c * TOK
                query = lax.rem(lax.broadcasted_iota(jnp.int32, s.shape, 1), TOK) + core * TOK
                s = jnp.where(key <= query, s, -1e30)
            s_ref[rows_at(z, c), :] = s
            peak = jnp.maximum(peak, partial_rows(s, jnp.max))
        return peak

    peak = score_step(chip, jnp.full((8, width), -1e30, f32), True)
    peak = lax.fori_loop(0, chip, lambda z, m: score_step(z, m, False), peak)
    peak = jnp.max(peak, axis=0, keepdims=True)

    def weight_step(z, carry):
        total, mixed = carry
        rel, hi = place(z)
        for c in range(2):
            e = jnp.exp2((s_ref[rows_at(z, c), :] - peak) * (SCALE * math.log2(math.e)))
            dp = dot(kv_ref[c, rel, hi, 1, :TOK, :], do, NT)
            s_ref[rows_at(z, c), :] = e
            dp_ref[rows_at(z, c), :] = dp
            total = total + partial_rows(e, jnp.sum)
            mixed = mixed + partial_rows(e * dp, jnp.sum)
        return total, mixed

    zero = jnp.zeros((8, width), f32)
    total, mixed = lax.fori_loop(0, chip + 1, weight_step, (zero, zero))
    inverse = 1.0 / jnp.sum(total, axis=0, keepdims=True)
    delta = jnp.sum(mixed, axis=0, keepdims=True) * inverse
    dqt_ref[...] = jnp.zeros_like(dqt_ref)

    def gradient_step(z, _):
        rel, hi = place(z)
        step = jnp.zeros(dqt_ref.shape, f32)
        for c in range(2):
            p = s_ref[rows_at(z, c), :] * inverse
            ds = (p * (dp_ref[rows_at(z, c), :] - delta)).astype(bf16)
            dkv_ref[c, rel, hi, 1] = dot(p.astype(bf16), do, NN).astype(bf16)
            dkv_ref[c, rel, hi, 0] = (dot(ds, q, NN) * SCALE).astype(bf16)
            step = step + dot(kv_ref[c, rel, hi, 0, :TOK, :], ds, TN)
        dqt_ref[...] += step
        return 0

    lax.fori_loop(0, chip + 1, gradient_step, 0)

    def clear_step(z, _):
        rel, hi = place(z)
        for c in range(2):
            for part in range(2):
                dkv_ref[c, rel, hi, part] = jnp.zeros((TOK, 128), bf16)
        return 0

    lax.fori_loop(chip + 1, CHIPS, clear_step, 0)
    dqt = dqt_ref[...] * SCALE
    for h in range(4):
        dq_ref[:, 128 * h : 128 * (h + 1)] = dqt[:, TOK * h : TOK * (h + 1)].T
    peak_ref[...] = jnp.broadcast_to(jnp.max(jnp.abs(dqt), keepdims=True), peak_ref.shape)


def spread_heads():
    shape = (SSM_HEADS, SSM_HEADS * SSM_DIM)
    row = lax.broadcasted_iota(jnp.int32, shape, 0)
    lane = lax.broadcasted_iota(jnp.int32, shape, 1)
    return (lane // SSM_DIM == row).astype(f32)


def running_decay(decay):
    row = lax.broadcasted_iota(jnp.int32, (TOK, TOK), 0)
    col = lax.broadcasted_iota(jnp.int32, (TOK, TOK), 1)
    lower = (col <= row).astype(f32)
    wide = dot(decay, spread_heads(), TN, HIGHEST)
    return dot(lower, wide, NN, HIGHEST)


def state_kernel(dy_ref, c_ref, decay_ref, out_ref):
    weighted = dy_ref[...].astype(f32) * jnp.exp(running_decay(decay_ref[...]))
    out_ref[...] = dot(weighted.astype(bf16), c_ref[...], TN).astype(bf16)


def scan_kernel(pos_ref, state_ref, total_ref, out_ref):
    lane_group = lax.rem(pos_ref[0], 4)
    pair = pos_ref[2]
    mine = (pos_ref[0] * 2 + pos_ref[1]) // 4
    lane = lax.broadcasted_iota(jnp.int32, (2, 128), 1)
    flow = jnp.zeros((16, 128), f32)
    for k in reversed(range(2 * CHIPS)):
        z, c = k // 2, k % 2
        out_ref[16 * k : 16 * (k + 1), :] = flow.astype(bf16)
        rel = lax.rem(z % 4 - lane_group + 4, 4)
        halves = total_ref[c, rel, z // 4, pair].astype(f32)
        total = jnp.sum(jnp.where(lane == mine, halves, 0.0), keepdims=True)
        flow = state_ref[16 * k : 16 * (k + 1), :].astype(f32) + jnp.exp(total) * flow


def ssm_kernel(dy_ref, b_ref, c_ref, decay_ref, skip_ref, flow_ref, dx_ref, peak_ref):
    decay = decay_ref[...]
    dy = dy_ref[...]
    wide = running_decay(decay)
    row = lax.broadcasted_iota(jnp.int32, (TOK, TOK), 0)
    col = lax.broadcasted_iota(jnp.int32, (TOK, TOK), 1)
    narrow = dot(decay, (row <= col).astype(f32), NN, HIGHEST)
    pairs = dot(b_ref[...], c_ref[...], NT)
    skip = jnp.sum(spread_heads() * skip_ref[...], axis=0, keepdims=True)
    carried = dot(b_ref[...], flow_ref[...], NT) * jnp.exp(wide[TOK - 1 :, :] - wide)
    rest = carried + skip * dy.astype(f32)
    top = jnp.zeros((1, 1), f32)
    for j in range(SSM_HEADS // 2):
        cols = slice(128 * j, 128 * (j + 1))
        both = dy[:, cols]
        out = rest[:, cols]
        for k in range(2):
            h = 2 * j + k
            span = narrow[h : h + 1, :] - wide[:, h * SSM_DIM : h * SSM_DIM + 1]
            weight = jnp.where(col >= row, jnp.exp(jnp.minimum(span, 0.0)), 0.0)
            kept = jnp.where(col // SSM_DIM == k, both, jnp.zeros_like(both))
            out = out + dot((pairs * weight).astype(bf16), kept, NN)
        dx_ref[:, cols] = out
        top = jnp.maximum(top, jnp.max(jnp.abs(out), keepdims=True))
    peak_ref[...] = jnp.broadcast_to(top, peak_ref.shape)


def call(body, out_shape, *args, scratch=(), scalars=0, name=None):
    specs = [pl.BlockSpec(memory_space=pltpu.SMEM)] * scalars
    specs += [pl.BlockSpec(memory_space=pltpu.VMEM)] * (len(args) - scalars)
    return pl.pallas_call(
        body,
        out_shape=out_shape,
        in_specs=specs,
        out_specs=jax.tree.map(lambda _: pl.BlockSpec(memory_space=pltpu.VMEM), out_shape),
        scratch_shapes=scratch,
        name=name,
    )(*args)


def swap_all(x, axes):
    return lax.all_to_all(x, axes, 0, 0, tiled=True)


def along_z(x, step):
    route = []
    for chip in range(CHIPS):
        for core in range(2):
            move = step if step != 2 or core == 0 else -2
            route.append((2 * chip + core, 2 * ((chip + move) % CHIPS) + core))
    return lax.ppermute(x, SEQ, route)


def on_device(queries, key_value, grad_out, ssm_grad, b_proj, c_proj, decay_log, skip_gain):
    chip = lax.axis_index(("hi", "lo"))
    core = lax.axis_index("c")
    pos = jnp.stack([chip, core, lax.axis_index("xp"), chip]).astype(jnp.int32)
    struct = jax.ShapeDtypeStruct

    total = jnp.sum(decay_log, axis=1)
    high = total.astype(bf16)
    low = (total - high.astype(f32)).astype(bf16)
    extra = jnp.zeros((EXTRA, 128), bf16).at[0, :SSM_HEADS].set(high).at[1, :SSM_HEADS].set(low)
    shard = jnp.concatenate([key_value, extra], axis=0)

    column = swap_all(jnp.tile(shard, (8, 1)), ("hi", "xp"))
    two = along_z(column, 2)
    after = along_z(column, -1)
    before = along_z(column, 1)
    state = call(state_kernel, struct((512, 128), bf16), ssm_grad, c_proj, decay_log, name="state")
    states = swap_all(state, SEQ)
    half = jnp.concatenate([column, after, two, before], axis=0)
    kv = swap_all(jnp.concatenate([half, half], axis=0), "c").reshape(2, 4, 4, 2, ROWS, 128)

    flows = call(
        scan_kernel, struct((512, 128), bf16), pos, states, kv[..., TOK : TOK + 2, :], scalars=1, name="scan"
    )
    flow = swap_all(flows, SEQ)

    dq, dkv, peak_q = call(
        attention_kernel,
        (struct((TOK, 512), f32), struct((2, 4, 4, 2, TOK, 128), bf16), struct((8, 128), f32)),
        pos,
        queries,
        grad_out,
        kv,
        scratch=(
            pltpu.VMEM((256 * CHIPS, 512), f32),
            pltpu.VMEM((256 * CHIPS, 512), f32),
            pltpu.VMEM((128, 512), f32),
        ),
        scalars=1,
        name="attention",
    )
    dx, peak_x = call(
        ssm_kernel,
        (struct((TOK, 512), f32), struct((8, 128), f32)),
        ssm_grad,
        b_proj,
        c_proj,
        decay_log,
        skip_gain.reshape(SSM_HEADS, 1),
        flow,
        name="ssm",
    )

    both = swap_all(dkv.reshape(2 * 4096, 128), "c").reshape(2, 4, 1024, 128).astype(f32)
    chip_sum = (both[0] + both[1]).astype(bf16)
    from_two = along_z(chip_sum[2], 2)
    from_before = along_z(chip_sum[1], 1)
    from_after = along_z(chip_sum[3], -1)
    near = (
        (chip_sum[0].astype(f32) + from_before.astype(f32)) + (from_after.astype(f32) + from_two.astype(f32))
    ).astype(bf16)
    far = swap_all(near, ("hi", "xp")).reshape(8, TOK, 128)
    dkv_own = jnp.sum(far.astype(f32), axis=0)

    lane = lax.broadcasted_iota(jnp.int32, (1, 128), 1)
    peak_kv = jnp.max(jnp.abs(dkv_own))
    peaks = jnp.where(lane == 0, peak_q[:1], jnp.where(lane == 1, peak_kv, peak_x[:1]))
    peaks = jnp.max(swap_all(jnp.tile(peaks, (32, 1)), SEQ), axis=0, keepdims=True)
    peaks = jnp.max(swap_all(jnp.tile(peaks, (16, 1)), HEAD), axis=0)
    return (
        (dq / (peaks[0] + EPSILON)).astype(bf16),
        (dkv_own / (peaks[1] + EPSILON)).astype(bf16),
        (dx / (peaks[2] + EPSILON)).astype(bf16),
    )


def solution(mesh):
    finer = Mesh(mesh.devices.reshape(SIZES), SEQ + HEAD)
    tokens = P(SEQ, HEAD)
    return jax.shard_map(
        on_device,
        mesh=finer,
        in_specs=(tokens, tokens, tokens, tokens, P(SEQ, None), P(SEQ, None), P(HEAD, SEQ), P(HEAD)),
        out_specs=(tokens, tokens, tokens),
        check_vma=False,
    )
```

```python
import math

import jax
import jax.numpy as jnp
from jax import lax
from jax.experimental import pallas as pl
from jax.experimental.pallas import tpu as pltpu
from jax.sharding import Mesh
from jax.sharding import PartitionSpec as P


SEQ = ("hi", "lo", "c")
HEAD = ("y", "xh", "xp")
SIZES = (4, 4, 2, 4, 2, 2)
CHIPS = 16
TOK = 128
SSM_HEADS = 8
SSM_DIM = 64
SCALE = 1.0 / math.sqrt(128)
EPSILON = 1e-6
HIGHEST = lax.Precision.HIGHEST
f32 = jnp.float32
bf16 = jnp.bfloat16


def dot(a, b, dims, precision=None):
    return lax.dot_general(a, b, (dims, ((), ())), precision=precision, preferred_element_type=f32)


NN = ((1,), (0,))
NT = ((1,), (1,))
TN = ((0,), (0,))


def heads_to_rows(x):
    return jnp.concatenate([x[:, 128 * h : 128 * (h + 1)] for h in range(4)], axis=0)


def attention_kernel(pos_ref, q_ref, do_ref, *refs):
    pieces, (dq_ref, dkv_ref, peak_ref, kv_ref, p_ref, dp_ref, outt_ref, dqt_ref, sems) = refs[:4], refs[4:]
    copies = [pltpu.make_async_copy(piece, kv_ref.at[r], sems.at[r]) for r, piece in enumerate(pieces)]
    for copy in copies:
        copy.start()
    chip, core = pos_ref[0], pos_ref[1]
    lane_group = lax.rem(chip, 4)
    q = heads_to_rows(q_ref[...])
    do = heads_to_rows(do_ref[...])
    width = q.shape[0]

    def place(z):
        return lax.rem(lax.rem(z, 4) - lane_group + 4, 4), z // 4

    def rows_at(z):
        return pl.ds(pl.multiple_of(z * 2 * TOK, 2 * TOK), 2 * TOK)

    def both_cores(z, part):
        rel, hi = place(z)
        return jnp.concatenate([kv_ref[rel, 0, hi, part], kv_ref[rel, 1, hi, part]], axis=0)

    def partial_rows(x, op):
        return op(x.reshape(2 * TOK // 8, 8, width), axis=0)

    def score_step(z, carry, masked):
        old, total = carry
        s = dot(both_cores(z, 0), q, NT) * SCALE
        if masked:
            key = lax.broadcasted_iota(jnp.int32, s.shape, 0)
            query = lax.rem(lax.broadcasted_iota(jnp.int32, s.shape, 1), TOK) + core * TOK
            s = jnp.where(key <= query, s, -1e30)
        top = jnp.maximum(old, jnp.max(partial_rows(s, jnp.max), axis=0, keepdims=True))
        p_ref[rows_at(z), :] = s
        return top, total * jnp.exp(old - top) + partial_rows(jnp.exp(s - top), jnp.sum)

    for copy in copies:
        copy.wait()
    carry = score_step(chip, (jnp.full((1, width), -1e30, f32), jnp.zeros((8, width), f32)), True)
    top, total = lax.fori_loop(0, chip, lambda z, c: score_step(z, c, False), carry)
    lse = top + jnp.log(jnp.sum(total, axis=0, keepdims=True))
    outt_ref[...] = jnp.zeros_like(outt_ref)
    dqt_ref[...] = jnp.zeros_like(dqt_ref)

    def output_step(z, _):
        rel, hi = place(z)
        p = jnp.exp(p_ref[rows_at(z), :] - lse)
        p_ref[rows_at(z), :] = p
        p_b = p.astype(bf16)
        values = both_cores(z, 1)
        outt_ref[...] += dot(values, p_b, TN)
        dp_ref[rows_at(z), :] = dot(values, do, NT)
        dv = dot(p_b, do, NN).astype(bf16)
        dkv_ref[0, rel, hi, 1] = dv[:TOK]
        dkv_ref[1, rel, hi, 1] = dv[TOK:]
        return 0

    lax.fori_loop(0, chip + 1, output_step, 0)
    dot_rows = jnp.concatenate([do_ref[:, 128 * h : 128 * (h + 1)].astype(f32).T for h in range(4)], axis=1)
    delta = jnp.sum(dot_rows * outt_ref[...].astype(bf16).astype(f32), axis=0, keepdims=True)

    def gradient_step(z, _):
        rel, hi = place(z)
        ds = (p_ref[rows_at(z), :] * (dp_ref[rows_at(z), :] - delta)).astype(bf16)
        dk = (dot(ds, q, NN) * SCALE).astype(bf16)
        dkv_ref[0, rel, hi, 0] = dk[:TOK]
        dkv_ref[1, rel, hi, 0] = dk[TOK:]
        dqt_ref[...] += dot(both_cores(z, 0), ds, TN)
        return 0

    lax.fori_loop(0, chip + 1, gradient_step, 0)

    def clear_step(z, _):
        rel, hi = place(z)
        for c in range(2):
            for part in range(2):
                dkv_ref[c, rel, hi, part] = jnp.zeros((TOK, 128), bf16)
        return 0

    lax.fori_loop(chip + 1, CHIPS, clear_step, 0)
    dqt = dqt_ref[...] * SCALE
    for h in range(4):
        dq_ref[:, 128 * h : 128 * (h + 1)] = dqt[:, TOK * h : TOK * (h + 1)].T
    peak_ref[...] = jnp.broadcast_to(jnp.max(jnp.abs(dqt), keepdims=True), peak_ref.shape)


def spread_heads():
    shape = (SSM_HEADS, SSM_HEADS * SSM_DIM)
    row = lax.broadcasted_iota(jnp.int32, shape, 0)
    lane = lax.broadcasted_iota(jnp.int32, shape, 1)
    return (lane // SSM_DIM == row).astype(f32)


def running_decay(decay):
    row = lax.broadcasted_iota(jnp.int32, (TOK, TOK), 0)
    col = lax.broadcasted_iota(jnp.int32, (TOK, TOK), 1)
    lower = (col <= row).astype(f32)
    wide = dot(decay, spread_heads(), TN, HIGHEST)
    return dot(lower, wide, NN, HIGHEST)


def state_kernel(dy_ref, c_ref, decay_ref, out_ref):
    wide = running_decay(decay_ref[...])
    weighted = dy_ref[...].astype(f32) * jnp.exp(wide)
    states = dot(weighted.astype(bf16), c_ref[...], TN).astype(bf16)
    row = lax.broadcasted_iota(jnp.int32, (8, 128), 0)
    for k in range(2 * CHIPS):
        head = k * 16 // SSM_DIM
        total = jnp.broadcast_to(wide[TOK - 1 :, head * SSM_DIM : head * SSM_DIM + 1], (8, 128))
        high = total.astype(bf16).astype(f32)
        out_ref[k, :16, :] = states[16 * k : 16 * (k + 1), :]
        out_ref[k, 16:, :] = jnp.where(row == 0, high, total - high).astype(bf16)


def scan_kernel(state_ref, out_ref):
    flow = jnp.zeros((16, 128), f32)
    for k in reversed(range(2 * CHIPS)):
        out_ref[k] = flow.astype(bf16)
        total = state_ref[k, 16:, :].astype(f32)
        flow = state_ref[k, :16, :].astype(f32) + jnp.exp(total[:1] + total[1:2]) * flow


def ssm_kernel(dy_ref, b_ref, c_ref, decay_ref, skip_ref, flow_ref, dx_ref, peak_ref):
    decay = decay_ref[...]
    dy = dy_ref[...]
    wide = running_decay(decay)
    row = lax.broadcasted_iota(jnp.int32, (TOK, TOK), 0)
    col = lax.broadcasted_iota(jnp.int32, (TOK, TOK), 1)
    narrow = dot(decay, (row <= col).astype(f32), NN, HIGHEST)
    pairs = dot(b_ref[...], c_ref[...], NT)
    skip = jnp.sum(spread_heads() * skip_ref[...], axis=0, keepdims=True)
    carried = dot(b_ref[...], flow_ref[...], NT) * jnp.exp(wide[TOK - 1 :, :] - wide)
    rest = carried + skip * dy.astype(f32)
    top = jnp.zeros((1, 1), f32)
    for j in range(SSM_HEADS // 2):
        cols = slice(128 * j, 128 * (j + 1))
        both = dy[:, cols]
        out = rest[:, cols]
        for k in range(2):
            h = 2 * j + k
            span = narrow[h : h + 1, :] - wide[:, h * SSM_DIM : h * SSM_DIM + 1]
            weight = jnp.where(col >= row, jnp.exp(jnp.minimum(span, 0.0)), 0.0)
            kept = jnp.where(col // SSM_DIM == k, both, jnp.zeros_like(both))
            out = out + dot((pairs * weight).astype(bf16), kept, NN)
        dx_ref[:, cols] = out
        top = jnp.maximum(top, jnp.max(jnp.abs(out), keepdims=True))
    peak_ref[...] = jnp.broadcast_to(top, peak_ref.shape)


def call(body, out_shape, *args, scratch=(), scalars=0, raw=0):
    specs = [pl.BlockSpec(memory_space=pltpu.SMEM)] * scalars
    specs += [pl.BlockSpec(memory_space=pltpu.VMEM)] * (len(args) - scalars - raw)
    specs += [pl.BlockSpec(memory_space=pl.ANY)] * raw
    return pl.pallas_call(
        body,
        out_shape=out_shape,
        in_specs=specs,
        out_specs=jax.tree.map(lambda _: pl.BlockSpec(memory_space=pltpu.VMEM), out_shape),
        scratch_shapes=scratch,
    )(*args)


def swap_all(x, axes):
    return lax.all_to_all(x, axes, 0, 0, tiled=True)


def along_z(x, step):
    route = []
    for chip in range(CHIPS):
        for core in range(2):
            move = step if step != 2 or core == 0 else -2
            route.append((2 * chip + core, 2 * ((chip + move) % CHIPS) + core))
    return lax.ppermute(x, SEQ, route)


def peak_kernel(far_ref, peak_q_ref, peak_x_ref, own_ref, out_ref):
    own = jnp.sum(far_ref[...].astype(f32), axis=0)
    own_ref[...] = own
    lane = lax.broadcasted_iota(jnp.int32, out_ref.shape, 1)
    peak_kv = jnp.max(jnp.abs(own), keepdims=True)
    out_ref[...] = jnp.where(lane == 0, peak_q_ref[:1], jnp.where(lane == 1, peak_kv, peak_x_ref[:1]))


def merge_kernel(peaks_ref, out_ref):
    out_ref[...] = jnp.broadcast_to(jnp.max(peaks_ref[...], axis=0, keepdims=True), out_ref.shape)


def scale_kernel(peaks_ref, dq_ref, dkv_ref, dx_ref, q_ref, kv_ref, x_ref):
    peaks = jnp.max(peaks_ref[...], axis=0, keepdims=True) + EPSILON
    q_ref[...] = (dq_ref[...] / peaks[:, 0:1]).astype(bf16)
    kv_ref[...] = (dkv_ref[...] / peaks[:, 1:2]).astype(bf16)
    x_ref[...] = (dx_ref[...] / peaks[:, 2:3]).astype(bf16)


def step(queries, key_value, grad_out, ssm_grad, b_proj, c_proj, decay_log, skip_gain):
    chip = lax.axis_index(("hi", "lo"))
    pos = jnp.stack([chip, lax.axis_index("c")]).astype(jnp.int32)
    struct = jax.ShapeDtypeStruct

    column = swap_all(jnp.tile(key_value, (8, 1)), ("hi", "xp"))
    two = along_z(column, 2)
    after = along_z(column, -1)
    before = along_z(column, 1)

    state = call(state_kernel, struct((2 * CHIPS, 24, 128), bf16), ssm_grad, c_proj, decay_log)
    states = swap_all(state, SEQ)
    flows = call(scan_kernel, struct((2 * CHIPS, 16, 128), bf16), states)
    flow = swap_all(flows, SEQ)

    pieces = []
    for piece in (column, after, two, before):
        pieces.append(lax.all_gather(piece, "c", axis=0, tiled=True).reshape(2, 4, 2, TOK, 128))
    dq, dkv, peak_q = call(
        attention_kernel,
        (struct((TOK, 512), f32), struct((2, 4, 4, 2, TOK, 128), bf16), struct((8, 128), f32)),
        pos,
        queries,
        grad_out,
        *pieces,
        scratch=(
            pltpu.VMEM((4, 2, 4, 2, TOK, 128), bf16),
            pltpu.VMEM((256 * CHIPS, 512), f32),
            pltpu.VMEM((256 * CHIPS, 512), f32),
            pltpu.VMEM((128, 512), f32),
            pltpu.VMEM((128, 512), f32),
            pltpu.SemaphoreType.DMA((4,)),
        ),
        scalars=1,
        raw=4,
    )

    both = swap_all(dkv.reshape(2 * 4096, 128), "c").reshape(2, 4, 1024, 128).astype(f32)
    chip_sum = (both[0] + both[1]).astype(bf16)
    from_two = along_z(chip_sum[2], 2)
    from_before = along_z(chip_sum[1], 1)
    from_after = along_z(chip_sum[3], -1)
    near = (
        (chip_sum[0].astype(f32) + from_before.astype(f32)) + (from_after.astype(f32) + from_two.astype(f32))
    ).astype(bf16)
    far = swap_all(near, ("hi", "xp")).reshape(8, TOK, 128)
    dx, peak_x = call(
        ssm_kernel,
        (struct((TOK, 512), f32), struct((8, 128), f32)),
        ssm_grad,
        b_proj,
        c_proj,
        decay_log,
        skip_gain.reshape(SSM_HEADS, 1),
        flow.reshape(512, 128),
    )

    dkv_own, peaks = call(peak_kernel, (struct((TOK, 128), f32), struct((32, 128), f32)), far, peak_q, peak_x)
    peaks = swap_all(peaks, SEQ)
    peaks = call(merge_kernel, struct((16, 128), f32), peaks)
    peaks = swap_all(peaks, HEAD)
    return call(
        scale_kernel,
        (struct((TOK, 512), bf16), struct((TOK, 128), bf16), struct((TOK, 512), bf16)),
        peaks,
        dq,
        dkv_own,
        dx,
    )


def solution(mesh):
    finer = Mesh(mesh.devices.reshape(SIZES), SEQ + HEAD)
    tokens = P(SEQ, HEAD)
    return jax.shard_map(
        step,
        mesh=finer,
        in_specs=(tokens, tokens, tokens, tokens, P(SEQ, None), P(SEQ, None), P(HEAD, SEQ), P(HEAD)),
        out_specs=(tokens, tokens, tokens),
        check_vma=False,
    )
```

```python
import math

import jax
import jax.numpy as jnp
from jax import lax
from jax.experimental import pallas as pl
from jax.experimental.pallas import tpu as pltpu
from jax.sharding import Mesh
from jax.sharding import PartitionSpec as P


SEQ = ("hi", "lo", "c")
HEAD = ("y", "xh", "xp")
SIZES = (4, 4, 2, 4, 2, 2)
CHIPS = 16
TOK = 128
SSM_HEADS = 8
SSM_DIM = 64
SCALE = 1.0 / math.sqrt(128)
EPSILON = 1e-6
HIGHEST = lax.Precision.HIGHEST
f32 = jnp.float32
bf16 = jnp.bfloat16


def dot(a, b, dims, precision=None):
    return lax.dot_general(a, b, (dims, ((), ())), precision=precision, preferred_element_type=f32)


NN = ((1,), (0,))
NT = ((1,), (1,))
TN = ((0,), (0,))


def heads_to_rows(x):
    return jnp.concatenate([x[:, 128 * h : 128 * (h + 1)] for h in range(4)], axis=0)


def attention_kernel(pos_ref, q_ref, do_ref, *refs):
    pieces, (dq_ref, dkv_ref, peak_ref, kv_ref, p_ref, dp_ref, outt_ref, dqt_ref, sems) = refs[:4], refs[4:]
    copies = [pltpu.make_async_copy(piece, kv_ref.at[r], sems.at[r]) for r, piece in enumerate(pieces)]
    for copy in copies:
        copy.start()
    chip, core = pos_ref[0], pos_ref[1]
    lane_group = lax.rem(chip, 4)
    q = heads_to_rows(q_ref[...])
    do = heads_to_rows(do_ref[...])
    width = q.shape[0]

    steps = chip // 2 + 1

    def place(z):
        return lax.rem(lax.rem(z, 4) - lane_group + 4, 4), z // 4

    def tiles(j):
        for z in (2 * j, 2 * j + 1):
            rel, hi = place(z)
            for c in range(2):
                yield rel, c, hi

    def rows_at(j):
        return pl.ds(pl.multiple_of(j * 4 * TOK, 4 * TOK), 4 * TOK)

    def keys_at(j, part):
        return jnp.concatenate([kv_ref[rel, c, hi, part] for rel, c, hi in tiles(j)], axis=0)

    def store_at(j, part, x):
        for k, (rel, c, hi) in enumerate(tiles(j)):
            dkv_ref[c, rel, hi, part] = x[TOK * k : TOK * (k + 1)]

    def partial_rows(x, op):
        return op(x.reshape(4 * TOK // 8, 8, width), axis=0)

    def score_step(j, carry, masked):
        old, total = carry
        s = dot(keys_at(j, 0), q, NT) * SCALE
        if masked:
            key = lax.broadcasted_iota(jnp.int32, s.shape, 0) + j * 4 * TOK
            query = lax.rem(lax.broadcasted_iota(jnp.int32, s.shape, 1), TOK) + (2 * chip + core) * TOK
            s = jnp.where(key <= query, s, -1e30)
        top = jnp.maximum(old, jnp.max(partial_rows(s, jnp.max), axis=0, keepdims=True))
        p_ref[rows_at(j), :] = s
        return top, total * jnp.exp(old - top) + partial_rows(jnp.exp(s - top), jnp.sum)

    for copy in copies:
        copy.wait()
    carry = score_step(steps - 1, (jnp.full((1, width), -1e30, f32), jnp.zeros((8, width), f32)), True)
    top, total = lax.fori_loop(0, steps - 1, lambda j, c: score_step(j, c, False), carry)
    lse = top + jnp.log(jnp.sum(total, axis=0, keepdims=True))
    outt_ref[...] = jnp.zeros_like(outt_ref)
    dqt_ref[...] = jnp.zeros_like(dqt_ref)

    def output_step(j, _):
        p = jnp.exp(p_ref[rows_at(j), :] - lse)
        p_ref[rows_at(j), :] = p
        p_b = p.astype(bf16)
        values = keys_at(j, 1)
        outt_ref[...] += dot(values, p_b, TN)
        dp_ref[rows_at(j), :] = dot(values, do, NT)
        store_at(j, 1, dot(p_b, do, NN).astype(bf16))
        return 0

    lax.fori_loop(0, steps, output_step, 0)
    dot_rows = jnp.concatenate([do_ref[:, 128 * h : 128 * (h + 1)].astype(f32).T for h in range(4)], axis=1)
    delta = jnp.sum(dot_rows * outt_ref[...].astype(bf16).astype(f32), axis=0, keepdims=True)

    def gradient_step(j, _):
        ds = (p_ref[rows_at(j), :] * (dp_ref[rows_at(j), :] - delta)).astype(bf16)
        store_at(j, 0, (dot(ds, q, NN) * SCALE).astype(bf16))
        dqt_ref[...] += dot(keys_at(j, 0), ds, TN)
        return 0

    lax.fori_loop(0, steps, gradient_step, 0)

    def clear_step(j, _):
        for part in range(2):
            store_at(j, part, jnp.zeros((4 * TOK, 128), bf16))
        return 0

    lax.fori_loop(steps, CHIPS // 2, clear_step, 0)
    dqt = dqt_ref[...] * SCALE
    for h in range(4):
        dq_ref[:, 128 * h : 128 * (h + 1)] = dqt[:, TOK * h : TOK * (h + 1)].T
    peak_ref[...] = jnp.broadcast_to(jnp.max(jnp.abs(dqt), keepdims=True), peak_ref.shape)


def spread_heads():
    shape = (SSM_HEADS, SSM_HEADS * SSM_DIM)
    row = lax.broadcasted_iota(jnp.int32, shape, 0)
    lane = lax.broadcasted_iota(jnp.int32, shape, 1)
    return (lane // SSM_DIM == row).astype(f32)


def running_decay(decay):
    row = lax.broadcasted_iota(jnp.int32, (TOK, TOK), 0)
    col = lax.broadcasted_iota(jnp.int32, (TOK, TOK), 1)
    lower = (col <= row).astype(f32)
    wide = dot(decay, spread_heads(), TN, HIGHEST)
    return dot(lower, wide, NN, HIGHEST)


def state_kernel(dy_ref, c_ref, decay_ref, out_ref):
    wide = running_decay(decay_ref[...])
    weighted = dy_ref[...].astype(f32) * jnp.exp(wide)
    states = dot(weighted.astype(bf16), c_ref[...], TN).astype(bf16)
    row = lax.broadcasted_iota(jnp.int32, (8, 128), 0)
    for k in range(2 * CHIPS):
        head = k * 16 // SSM_DIM
        total = jnp.broadcast_to(wide[TOK - 1 :, head * SSM_DIM : head * SSM_DIM + 1], (8, 128))
        high = total.astype(bf16).astype(f32)
        out_ref[k, :16, :] = states[16 * k : 16 * (k + 1), :]
        out_ref[k, 16:, :] = jnp.where(row == 0, high, total - high).astype(bf16)


def scan_kernel(state_ref, out_ref):
    flow = jnp.zeros((16, 128), f32)
    for k in reversed(range(2 * CHIPS)):
        out_ref[k] = flow.astype(bf16)
        total = state_ref[k, 16:, :].astype(f32)
        flow = state_ref[k, :16, :].astype(f32) + jnp.exp(total[:1] + total[1:2]) * flow


def ssm_kernel(dy_ref, b_ref, c_ref, decay_ref, skip_ref, flow_ref, dx_ref, peak_ref):
    decay = decay_ref[...]
    dy = dy_ref[...]
    wide = running_decay(decay)
    row = lax.broadcasted_iota(jnp.int32, (TOK, TOK), 0)
    col = lax.broadcasted_iota(jnp.int32, (TOK, TOK), 1)
    narrow = dot(decay, (row <= col).astype(f32), NN, HIGHEST)
    pairs = dot(b_ref[...], c_ref[...], NT)
    skip = jnp.sum(spread_heads() * skip_ref[...], axis=0, keepdims=True)
    carried = dot(b_ref[...], flow_ref[...], NT) * jnp.exp(wide[TOK - 1 :, :] - wide)
    rest = carried + skip * dy.astype(f32)
    top = jnp.zeros((1, 1), f32)
    for j in range(SSM_HEADS // 2):
        cols = slice(128 * j, 128 * (j + 1))
        both = dy[:, cols]
        out = rest[:, cols]
        for k in range(2):
            h = 2 * j + k
            span = narrow[h : h + 1, :] - wide[:, h * SSM_DIM : h * SSM_DIM + 1]
            weight = jnp.where(col >= row, jnp.exp(jnp.minimum(span, 0.0)), 0.0)
            kept = jnp.where(col // SSM_DIM == k, both, jnp.zeros_like(both))
            out = out + dot((pairs * weight).astype(bf16), kept, NN)
        dx_ref[:, cols] = out
        top = jnp.maximum(top, jnp.max(jnp.abs(out), keepdims=True))
    peak_ref[...] = jnp.broadcast_to(top, peak_ref.shape)


def call(body, out_shape, *args, scratch=(), scalars=0, raw=0):
    specs = [pl.BlockSpec(memory_space=pltpu.SMEM)] * scalars
    specs += [pl.BlockSpec(memory_space=pltpu.VMEM)] * (len(args) - scalars - raw)
    specs += [pl.BlockSpec(memory_space=pl.ANY)] * raw
    return pl.pallas_call(
        body,
        out_shape=out_shape,
        in_specs=specs,
        out_specs=jax.tree.map(lambda _: pl.BlockSpec(memory_space=pltpu.VMEM), out_shape),
        scratch_shapes=scratch,
    )(*args)


def swap_all(x, axes):
    return lax.all_to_all(x, axes, 0, 0, tiled=True)


def along_z(x, step):
    route = []
    for chip in range(CHIPS):
        for core in range(2):
            move = step if step != 2 or core == 0 else -2
            route.append((2 * chip + core, 2 * ((chip + move) % CHIPS) + core))
    return lax.ppermute(x, SEQ, route)


def peak_kernel(far_ref, peak_q_ref, peak_x_ref, own_ref, out_ref):
    own = jnp.sum(far_ref[...].astype(f32), axis=0)
    own_ref[...] = own
    lane = lax.broadcasted_iota(jnp.int32, out_ref.shape, 1)
    peak_kv = jnp.max(jnp.abs(own), keepdims=True)
    out_ref[...] = jnp.where(lane == 0, peak_q_ref[:1], jnp.where(lane == 1, peak_kv, peak_x_ref[:1]))


def merge_kernel(peaks_ref, out_ref):
    out_ref[...] = jnp.broadcast_to(jnp.max(peaks_ref[...], axis=0, keepdims=True), out_ref.shape)


def scale_kernel(peaks_ref, dq_ref, dkv_ref, dx_ref, q_ref, kv_ref, x_ref):
    peaks = jnp.max(peaks_ref[...], axis=0, keepdims=True) + EPSILON
    q_ref[...] = (dq_ref[...] / peaks[:, 0:1]).astype(bf16)
    kv_ref[...] = (dkv_ref[...] / peaks[:, 1:2]).astype(bf16)
    x_ref[...] = (dx_ref[...] / peaks[:, 2:3]).astype(bf16)


def step(queries, key_value, grad_out, ssm_grad, b_proj, c_proj, decay_log, skip_gain):
    chip = lax.axis_index(("hi", "lo"))
    pos = jnp.stack([chip, lax.axis_index("c")]).astype(jnp.int32)
    struct = jax.ShapeDtypeStruct

    column = swap_all(jnp.tile(key_value, (8, 1)), ("hi", "xp"))
    two = along_z(column, 2)
    after = along_z(column, -1)
    before = along_z(column, 1)

    state = call(state_kernel, struct((2 * CHIPS, 24, 128), bf16), ssm_grad, c_proj, decay_log)
    states = swap_all(state, SEQ)
    flows = call(scan_kernel, struct((2 * CHIPS, 16, 128), bf16), states)
    flow = swap_all(flows, SEQ)

    pieces = []
    for piece in (column, after, two, before):
        pieces.append(lax.all_gather(piece, "c", axis=0, tiled=True).reshape(2, 4, 2, TOK, 128))
    dq, dkv, peak_q = call(
        attention_kernel,
        (struct((TOK, 512), f32), struct((2, 4, 4, 2, TOK, 128), bf16), struct((8, 128), f32)),
        pos,
        queries,
        grad_out,
        *pieces,
        scratch=(
            pltpu.VMEM((4, 2, 4, 2, TOK, 128), bf16),
            pltpu.VMEM((256 * CHIPS, 512), f32),
            pltpu.VMEM((256 * CHIPS, 512), f32),
            pltpu.VMEM((128, 512), f32),
            pltpu.VMEM((128, 512), f32),
            pltpu.SemaphoreType.DMA((4,)),
        ),
        scalars=1,
        raw=4,
    )

    both = swap_all(dkv.reshape(2 * 4096, 128), "c").reshape(2, 4, 1024, 128).astype(f32)
    chip_sum = (both[0] + both[1]).astype(bf16)
    from_two = along_z(chip_sum[2], 2)
    from_before = along_z(chip_sum[1], 1)
    from_after = along_z(chip_sum[3], -1)
    near = (
        (chip_sum[0].astype(f32) + from_before.astype(f32)) + (from_after.astype(f32) + from_two.astype(f32))
    ).astype(bf16)
    far = swap_all(near, ("hi", "xp")).reshape(8, TOK, 128)
    dx, peak_x = call(
        ssm_kernel,
        (struct((TOK, 512), f32), struct((8, 128), f32)),
        ssm_grad,
        b_proj,
        c_proj,
        decay_log,
        skip_gain.reshape(SSM_HEADS, 1),
        flow.reshape(512, 128),
    )

    dkv_own, peaks = call(peak_kernel, (struct((TOK, 128), f32), struct((32, 128), f32)), far, peak_q, peak_x)
    peaks = swap_all(peaks, SEQ)
    peaks = call(merge_kernel, struct((16, 128), f32), peaks)
    peaks = swap_all(peaks, HEAD)
    return call(
        scale_kernel,
        (struct((TOK, 512), bf16), struct((TOK, 128), bf16), struct((TOK, 512), bf16)),
        peaks,
        dq,
        dkv_own,
        dx,
    )


def solution(mesh):
    finer = Mesh(mesh.devices.reshape(SIZES), SEQ + HEAD)
    tokens = P(SEQ, HEAD)
    return jax.shard_map(
        step,
        mesh=finer,
        in_specs=(tokens, tokens, tokens, tokens, P(SEQ, None), P(SEQ, None), P(HEAD, SEQ), P(HEAD)),
        out_specs=(tokens, tokens, tokens),
        check_vma=False,
    )
```

```python
import math

import jax
import jax.numpy as jnp
from jax import lax
from jax.experimental import pallas as pl
from jax.experimental.pallas import tpu as pltpu
from jax.sharding import Mesh
from jax.sharding import PartitionSpec as P


SEQ = ("hi", "lo", "c")
HEAD = ("y", "xh", "xp")
SIZES = (4, 4, 2, 4, 2, 2)
CHIPS = 16
TOK = 128
SSM_HEADS = 8
SSM_DIM = 64
SCALE = 1.0 / math.sqrt(128)
EPSILON = 1e-6
HIGHEST = lax.Precision.HIGHEST
f32 = jnp.float32
bf16 = jnp.bfloat16


def dot(a, b, dims, precision=None):
    return lax.dot_general(a, b, (dims, ((), ())), precision=precision, preferred_element_type=f32)


NN = ((1,), (0,))
NT = ((1,), (1,))
TN = ((0,), (0,))


def heads_to_rows(x):
    return jnp.concatenate([x[:, 128 * h : 128 * (h + 1)] for h in range(4)], axis=0)


def attention_kernel(pos_ref, q_ref, do_ref, *refs):
    pieces, (dq_ref, dkv_ref, peak_ref, kv_ref, p_ref, dp_ref, outt_ref, dqt_ref, sems) = refs[:4], refs[4:]
    copies = [pltpu.make_async_copy(piece, kv_ref.at[r], sems.at[r]) for r, piece in enumerate(pieces)]
    for copy in copies:
        copy.start()
    chip, core = pos_ref[0], pos_ref[1]
    lane_group = lax.rem(chip, 4)
    q = heads_to_rows(q_ref[...])
    do = heads_to_rows(do_ref[...])
    width = q.shape[0]

    steps = chip // 2 + 1

    def place(z):
        return lax.rem(lax.rem(z, 4) - lane_group + 4, 4), z // 4

    def tiles(j):
        for z in (2 * j, 2 * j + 1):
            rel, hi = place(z)
            for c in range(2):
                yield rel, c, hi

    def rows_at(j):
        return pl.ds(pl.multiple_of(j * 4 * TOK, 4 * TOK), 4 * TOK)

    def keys_at(j, part):
        return jnp.concatenate([kv_ref[rel, c, hi, part] for rel, c, hi in tiles(j)], axis=0)

    def store_at(j, part, x):
        for k, (rel, c, hi) in enumerate(tiles(j)):
            dkv_ref[c, rel, hi, part] = x[TOK * k : TOK * (k + 1)]

    def partial_rows(x, op):
        return op(x.reshape(4 * TOK // 8, 8, width), axis=0)

    def score_step(j, carry, masked):
        old, total = carry
        s = dot(keys_at(j, 0), q, NT) * SCALE
        if masked:
            key = lax.broadcasted_iota(jnp.int32, s.shape, 0) + j * 4 * TOK
            query = lax.rem(lax.broadcasted_iota(jnp.int32, s.shape, 1), TOK) + (2 * chip + core) * TOK
            s = jnp.where(key <= query, s, -1e30)
        top = jnp.maximum(old, jnp.max(partial_rows(s, jnp.max), axis=0, keepdims=True))
        p_ref[rows_at(j), :] = s
        return top, total * jnp.exp(old - top) + partial_rows(jnp.exp(s - top), jnp.sum)

    for copy in copies:
        copy.wait()
    carry = score_step(steps - 1, (jnp.full((1, width), -1e30, f32), jnp.zeros((8, width), f32)), True)
    top, total = lax.fori_loop(0, steps - 1, lambda j, c: score_step(j, c, False), carry)
    lse = top + jnp.log(jnp.sum(total, axis=0, keepdims=True))
    outt_ref[...] = jnp.zeros_like(outt_ref)
    dqt_ref[...] = jnp.zeros_like(dqt_ref)

    def output_step(j, _):
        p = jnp.exp(p_ref[rows_at(j), :] - lse)
        p_ref[rows_at(j), :] = p
        p_b = p.astype(bf16)
        values = keys_at(j, 1)
        outt_ref[...] += dot(values, p_b, TN)
        dp_ref[rows_at(j), :] = dot(values, do, NT)
        store_at(j, 1, dot(p_b, do, NN).astype(bf16))
        return 0

    lax.fori_loop(0, steps, output_step, 0)
    dot_rows = jnp.concatenate([do_ref[:, 128 * h : 128 * (h + 1)].astype(f32).T for h in range(4)], axis=1)
    delta = jnp.sum(dot_rows * outt_ref[...].astype(bf16).astype(f32), axis=0, keepdims=True)

    def gradient_step(j, _):
        ds = (p_ref[rows_at(j), :] * (dp_ref[rows_at(j), :] - delta)).astype(bf16)
        store_at(j, 0, (dot(ds, q, NN) * SCALE).astype(bf16))
        dqt_ref[...] += dot(keys_at(j, 0), ds, TN)
        return 0

    lax.fori_loop(0, steps, gradient_step, 0)

    def clear_step(j, _):
        for part in range(2):
            store_at(j, part, jnp.zeros((4 * TOK, 128), bf16))
        return 0

    lax.fori_loop(steps, CHIPS // 2, clear_step, 0)
    dqt = dqt_ref[...] * SCALE
    for h in range(4):
        dq_ref[:, 128 * h : 128 * (h + 1)] = dqt[:, TOK * h : TOK * (h + 1)].T
    peak_ref[...] = jnp.broadcast_to(jnp.max(jnp.abs(dqt), keepdims=True), peak_ref.shape)


def spread_heads():
    shape = (SSM_HEADS, SSM_HEADS * SSM_DIM)
    row = lax.broadcasted_iota(jnp.int32, shape, 0)
    lane = lax.broadcasted_iota(jnp.int32, shape, 1)
    return (lane // SSM_DIM == row).astype(f32)


def running_decay(decay):
    row = lax.broadcasted_iota(jnp.int32, (TOK, TOK), 0)
    col = lax.broadcasted_iota(jnp.int32, (TOK, TOK), 1)
    lower = (col <= row).astype(f32)
    wide = dot(decay, spread_heads(), TN, HIGHEST)
    return dot(lower, wide, NN, HIGHEST)


def state_kernel(dy_ref, c_ref, decay_ref, out_ref):
    wide = running_decay(decay_ref[...])
    weighted = dy_ref[...].astype(f32) * jnp.exp(wide)
    states = dot(weighted.astype(bf16), c_ref[...], TN).astype(bf16)
    row = lax.broadcasted_iota(jnp.int32, (8, 128), 0)
    for k in range(2 * CHIPS):
        head = k * 16 // SSM_DIM
        total = jnp.broadcast_to(wide[TOK - 1 :, head * SSM_DIM : head * SSM_DIM + 1], (8, 128))
        high = total.astype(bf16).astype(f32)
        out_ref[k, :16, :] = states[16 * k : 16 * (k + 1), :]
        out_ref[k, 16:, :] = jnp.where(row == 0, high, total - high).astype(bf16)


def scan_kernel(state_ref, out_ref):
    flow = jnp.zeros((16, 128), f32)
    for k in reversed(range(2 * CHIPS)):
        out_ref[k] = flow.astype(bf16)
        total = state_ref[k, 16:, :].astype(f32)
        flow = state_ref[k, :16, :].astype(f32) + jnp.exp(total[:1] + total[1:2]) * flow


def ssm_kernel(dy_ref, b_ref, c_ref, decay_ref, skip_ref, flow_ref, dx_ref, peak_ref):
    decay = decay_ref[...]
    dy = dy_ref[...]
    wide = running_decay(decay)
    row = lax.broadcasted_iota(jnp.int32, (TOK, TOK), 0)
    col = lax.broadcasted_iota(jnp.int32, (TOK, TOK), 1)
    narrow = dot(decay, (row <= col).astype(f32), NN, HIGHEST)
    pairs = dot(b_ref[...], c_ref[...], NT)
    skip = jnp.sum(spread_heads() * skip_ref[...], axis=0, keepdims=True)
    carried = dot(b_ref[...], flow_ref[...], NT) * jnp.exp(wide[TOK - 1 :, :] - wide)
    rest = carried + skip * dy.astype(f32)
    top = jnp.zeros((1, 1), f32)
    for j in range(SSM_HEADS // 2):
        cols = slice(128 * j, 128 * (j + 1))
        both = dy[:, cols]
        out = rest[:, cols]
        for k in range(2):
            h = 2 * j + k
            span = narrow[h : h + 1, :] - wide[:, h * SSM_DIM : h * SSM_DIM + 1]
            weight = jnp.where(col >= row, jnp.exp(jnp.minimum(span, 0.0)), 0.0)
            kept = jnp.where(col // SSM_DIM == k, both, jnp.zeros_like(both))
            out = out + dot((pairs * weight).astype(bf16), kept, NN)
        dx_ref[:, cols] = out
        top = jnp.maximum(top, jnp.max(jnp.abs(out), keepdims=True))
    peak_ref[...] = jnp.broadcast_to(top, peak_ref.shape)


def call(body, out_shape, *args, scratch=(), scalars=0, raw=0):
    specs = [pl.BlockSpec(memory_space=pltpu.SMEM)] * scalars
    specs += [pl.BlockSpec(memory_space=pltpu.VMEM)] * (len(args) - scalars - raw)
    specs += [pl.BlockSpec(memory_space=pl.ANY)] * raw
    return pl.pallas_call(
        body,
        out_shape=out_shape,
        in_specs=specs,
        out_specs=jax.tree.map(lambda _: pl.BlockSpec(memory_space=pltpu.VMEM), out_shape),
        scratch_shapes=scratch,
    )(*args)


def swap_all(x, axes):
    return lax.all_to_all(x, axes, 0, 0, tiled=True)


def along_z(x, step):
    route = []
    for chip in range(CHIPS):
        for core in range(2):
            move = step if step != 2 or core == 0 else -2
            route.append((2 * chip + core, 2 * ((chip + move) % CHIPS) + core))
    return lax.ppermute(x, SEQ, route)


def scale_kernel(peaks_ref, dq_ref, dkv_ref, dx_ref, q_ref, kv_ref, x_ref):
    peaks = jnp.max(peaks_ref[...], axis=0, keepdims=True) + EPSILON
    q_ref[...] = (dq_ref[...] / peaks[:, 0:1]).astype(bf16)
    kv_ref[...] = (dkv_ref[...] / peaks[:, 1:2]).astype(bf16)
    x_ref[...] = (dx_ref[...] / peaks[:, 2:3]).astype(bf16)


def step(queries, key_value, grad_out, ssm_grad, b_proj, c_proj, decay_log, skip_gain):
    chip = lax.axis_index(("hi", "lo"))
    pos = jnp.stack([chip, lax.axis_index("c")]).astype(jnp.int32)
    struct = jax.ShapeDtypeStruct

    column = swap_all(jnp.tile(key_value, (8, 1)), ("hi", "xp"))
    two = along_z(column, 2)
    after = along_z(column, -1)
    before = along_z(column, 1)

    state = call(state_kernel, struct((2 * CHIPS, 24, 128), bf16), ssm_grad, c_proj, decay_log)
    states = swap_all(state, SEQ)
    flows = call(scan_kernel, struct((2 * CHIPS, 16, 128), bf16), states)
    flow = swap_all(flows, SEQ)

    pieces = []
    for piece in (column, after, two, before):
        pieces.append(lax.all_gather(piece, "c", axis=0, tiled=True).reshape(2, 4, 2, TOK, 128))
    dq, dkv, peak_q = call(
        attention_kernel,
        (struct((TOK, 512), f32), struct((2, 4, 4, 2, TOK, 128), bf16), struct((8, 128), f32)),
        pos,
        queries,
        grad_out,
        *pieces,
        scratch=(
            pltpu.VMEM((4, 2, 4, 2, TOK, 128), bf16),
            pltpu.VMEM((256 * CHIPS, 512), f32),
            pltpu.VMEM((256 * CHIPS, 512), f32),
            pltpu.VMEM((128, 512), f32),
            pltpu.VMEM((128, 512), f32),
            pltpu.SemaphoreType.DMA((4,)),
        ),
        scalars=1,
        raw=4,
    )

    both = swap_all(dkv.reshape(2 * 4096, 128), "c").reshape(2, 4, 1024, 128).astype(f32)
    chip_sum = (both[0] + both[1]).astype(bf16)
    from_two = along_z(chip_sum[2], 2)
    from_before = along_z(chip_sum[1], 1)
    from_after = along_z(chip_sum[3], -1)
    near = (
        (chip_sum[0].astype(f32) + from_before.astype(f32)) + (from_after.astype(f32) + from_two.astype(f32))
    ).astype(bf16)
    far = swap_all(near, ("hi", "xp")).reshape(8, TOK, 128)
    dx, peak_x = call(
        ssm_kernel,
        (struct((TOK, 512), f32), struct((8, 128), f32)),
        ssm_grad,
        b_proj,
        c_proj,
        decay_log,
        skip_gain.reshape(SSM_HEADS, 1),
        flow.reshape(512, 128),
    )

    dkv_own = jnp.sum(far.astype(f32), axis=0)
    lane = lax.broadcasted_iota(jnp.int32, (1, 128), 1)
    early = jnp.where(lane == 0, peak_q[:1], peak_x[:1])
    early = lax.optimization_barrier(early)
    peaks = jnp.where(lane == 1, jnp.max(jnp.abs(dkv_own)), early)
    peaks = jnp.max(swap_all(jnp.tile(peaks, (32, 1)), SEQ), axis=0, keepdims=True)
    peaks = swap_all(jnp.tile(peaks, (16, 1)), HEAD)
    return call(
        scale_kernel,
        (struct((TOK, 512), bf16), struct((TOK, 128), bf16), struct((TOK, 512), bf16)),
        peaks,
        dq,
        dkv_own,
        dx,
    )


def solution(mesh):
    finer = Mesh(mesh.devices.reshape(SIZES), SEQ + HEAD)
    tokens = P(SEQ, HEAD)
    return jax.shard_map(
        step,
        mesh=finer,
        in_specs=(tokens, tokens, tokens, tokens, P(SEQ, None), P(SEQ, None), P(HEAD, SEQ), P(HEAD)),
        out_specs=(tokens, tokens, tokens),
        check_vma=False,
    )
```

```python
import math

import jax
import jax.numpy as jnp
from jax import lax
from jax.experimental import pallas as pl
from jax.experimental.pallas import tpu as pltpu
from jax.sharding import Mesh
from jax.sharding import PartitionSpec as P


SEQ = ("z", "c")
HEAD = ("y", "xh", "xp")
SIZES = (16, 2, 4, 2, 2)
NEAR = (-2, -1, 0, 1, 2)
CHIPS = 16
TOK = 128
SSM_HEADS = 8
SSM_DIM = 64
SCALE = 1.0 / math.sqrt(128)
EPSILON = 1e-6
HIGHEST = lax.Precision.HIGHEST
f32 = jnp.float32
bf16 = jnp.bfloat16


def dot(a, b, dims, precision=None):
    return lax.dot_general(a, b, (dims, ((), ())), precision=precision, preferred_element_type=f32)


NN = ((1,), (0,))
NT = ((1,), (1,))
TN = ((0,), (0,))


def heads_to_rows(x):
    return jnp.concatenate([x[:, 128 * h : 128 * (h + 1)] for h in range(4)], axis=0)


def attention_kernel(pos_ref, q_ref, do_ref, *refs):
    pieces, (dq_ref, dkv_ref, peak_ref, kv_ref, p_ref, dp_ref, outt_ref, dqt_ref, sems) = refs[:6], refs[6:]
    copies = []
    for k, piece in enumerate(pieces):
        count = piece.shape[0]
        copies.append(pltpu.make_async_copy(piece, kv_ref.at[pl.ds(12 * k, count)], sems.at[k]))
    for copy in copies:
        copy.start()
    chip, core = pos_ref[0], pos_ref[1]
    q = heads_to_rows(q_ref[...])
    do = heads_to_rows(do_ref[...])
    width = q.shape[0]

    steps = chip // 2 + 1

    def tiles(j):
        for z in (2 * j, 2 * j + 1):
            k = lax.rem(z - chip + 7 + CHIPS, CHIPS)
            near, far = lax.rem(k, 5), k // 5
            for c in range(2):
                held = jnp.where(k == 15, 60 + 2 * c, 12 * near + 6 * c + 2 * far)
                yield held, 2 * CHIPS * c + 2 * jnp.where(k == 15, 15, 3 * near + far)

    def rows_at(j):
        return pl.ds(pl.multiple_of(j * 4 * TOK, 4 * TOK), 4 * TOK)

    def keys_at(j, part):
        return jnp.concatenate([kv_ref[held + part] for held, _ in tiles(j)], axis=0)

    def store_at(j, part, x):
        for k, (_, out) in enumerate(tiles(j)):
            dkv_ref[out + part] = x[TOK * k : TOK * (k + 1)]

    def partial_rows(x, op):
        return op(x.reshape(4 * TOK // 8, 8, width), axis=0)

    def score_step(j, carry, masked):
        old, total = carry
        s = dot(keys_at(j, 0), q, NT) * SCALE
        if masked:
            key = lax.broadcasted_iota(jnp.int32, s.shape, 0) + j * 4 * TOK
            query = lax.rem(lax.broadcasted_iota(jnp.int32, s.shape, 1), TOK) + (2 * chip + core) * TOK
            s = jnp.where(key <= query, s, -1e30)
        top = jnp.maximum(old, jnp.max(partial_rows(s, jnp.max), axis=0, keepdims=True))
        p_ref[rows_at(j), :] = s
        return top, total * jnp.exp(old - top) + partial_rows(jnp.exp(s - top), jnp.sum)

    for copy in copies:
        copy.wait()
    carry = score_step(steps - 1, (jnp.full((1, width), -1e30, f32), jnp.zeros((8, width), f32)), True)
    top, total = lax.fori_loop(0, steps - 1, lambda j, c: score_step(j, c, False), carry)
    lse = top + jnp.log(jnp.sum(total, axis=0, keepdims=True))
    outt_ref[...] = jnp.zeros_like(outt_ref)
    dqt_ref[...] = jnp.zeros_like(dqt_ref)

    def output_step(j, _):
        p = jnp.exp(p_ref[rows_at(j), :] - lse)
        p_ref[rows_at(j), :] = p
        p_b = p.astype(bf16)
        values = keys_at(j, 1)
        outt_ref[...] += dot(values, p_b, TN)
        dp_ref[rows_at(j), :] = dot(values, do, NT)
        store_at(j, 1, dot(p_b, do, NN).astype(bf16))
        return 0

    lax.fori_loop(0, steps, output_step, 0)
    dot_rows = jnp.concatenate([do_ref[:, 128 * h : 128 * (h + 1)].astype(f32).T for h in range(4)], axis=1)
    delta = jnp.sum(dot_rows * outt_ref[...].astype(bf16).astype(f32), axis=0, keepdims=True)

    def gradient_step(j, _):
        ds = (p_ref[rows_at(j), :] * (dp_ref[rows_at(j), :] - delta)).astype(bf16)
        store_at(j, 0, (dot(ds, q, NN) * SCALE).astype(bf16))
        dqt_ref[...] += dot(keys_at(j, 0), ds, TN)
        return 0

    lax.fori_loop(0, steps, gradient_step, 0)

    def clear_step(j, _):
        for part in range(2):
            store_at(j, part, jnp.zeros((4 * TOK, 128), bf16))
        return 0

    lax.fori_loop(steps, CHIPS // 2, clear_step, 0)
    dqt = dqt_ref[...] * SCALE
    for h in range(4):
        dq_ref[:, 128 * h : 128 * (h + 1)] = dqt[:, TOK * h : TOK * (h + 1)].T
    peak_ref[...] = jnp.broadcast_to(jnp.max(jnp.abs(dqt), keepdims=True), peak_ref.shape)


def spread_heads():
    shape = (SSM_HEADS, SSM_HEADS * SSM_DIM)
    row = lax.broadcasted_iota(jnp.int32, shape, 0)
    lane = lax.broadcasted_iota(jnp.int32, shape, 1)
    return (lane // SSM_DIM == row).astype(f32)


def running_decay(decay):
    row = lax.broadcasted_iota(jnp.int32, (TOK, TOK), 0)
    col = lax.broadcasted_iota(jnp.int32, (TOK, TOK), 1)
    lower = (col <= row).astype(f32)
    wide = dot(decay, spread_heads(), TN, HIGHEST)
    return dot(lower, wide, NN, HIGHEST)


def state_kernel(dy_ref, c_ref, decay_ref, out_ref):
    wide = running_decay(decay_ref[...])
    weighted = dy_ref[...].astype(f32) * jnp.exp(wide)
    states = dot(weighted.astype(bf16), c_ref[...], TN).astype(bf16)
    row = lax.broadcasted_iota(jnp.int32, (8, 128), 0)
    for k in range(2 * CHIPS):
        head = k * 16 // SSM_DIM
        total = jnp.broadcast_to(wide[TOK - 1 :, head * SSM_DIM : head * SSM_DIM + 1], (8, 128))
        high = total.astype(bf16).astype(f32)
        out_ref[k, :16, :] = states[16 * k : 16 * (k + 1), :]
        out_ref[k, 16:, :] = jnp.where(row == 0, high, total - high).astype(bf16)


def scan_kernel(state_ref, out_ref):
    flow = jnp.zeros((16, 128), f32)
    for k in reversed(range(2 * CHIPS)):
        out_ref[k] = flow.astype(bf16)
        total = state_ref[k, 16:, :].astype(f32)
        flow = state_ref[k, :16, :].astype(f32) + jnp.exp(total[:1] + total[1:2]) * flow


def ssm_kernel(dy_ref, b_ref, c_ref, decay_ref, skip_ref, flow_ref, dx_ref, peak_ref):
    decay = decay_ref[...]
    dy = dy_ref[...]
    wide = running_decay(decay)
    row = lax.broadcasted_iota(jnp.int32, (TOK, TOK), 0)
    col = lax.broadcasted_iota(jnp.int32, (TOK, TOK), 1)
    narrow = dot(decay, (row <= col).astype(f32), NN, HIGHEST)
    pairs = dot(b_ref[...], c_ref[...], NT)
    skip = jnp.sum(spread_heads() * skip_ref[...], axis=0, keepdims=True)
    carried = dot(b_ref[...], flow_ref[...], NT) * jnp.exp(wide[TOK - 1 :, :] - wide)
    rest = carried + skip * dy.astype(f32)
    top = jnp.zeros((1, 1), f32)
    for j in range(SSM_HEADS // 2):
        cols = slice(128 * j, 128 * (j + 1))
        both = dy[:, cols]
        out = rest[:, cols]
        for k in range(2):
            h = 2 * j + k
            span = narrow[h : h + 1, :] - wide[:, h * SSM_DIM : h * SSM_DIM + 1]
            weight = jnp.where(col >= row, jnp.exp(jnp.minimum(span, 0.0)), 0.0)
            kept = jnp.where(col // SSM_DIM == k, both, jnp.zeros_like(both))
            out = out + dot((pairs * weight).astype(bf16), kept, NN)
        dx_ref[:, cols] = out
        top = jnp.maximum(top, jnp.max(jnp.abs(out), keepdims=True))
    peak_ref[...] = jnp.broadcast_to(top, peak_ref.shape)


def call(body, out_shape, *args, scratch=(), scalars=0, raw=0):
    specs = [pl.BlockSpec(memory_space=pltpu.SMEM)] * scalars
    specs += [pl.BlockSpec(memory_space=pltpu.VMEM)] * (len(args) - scalars - raw)
    specs += [pl.BlockSpec(memory_space=pl.ANY)] * raw
    return pl.pallas_call(
        body,
        out_shape=out_shape,
        in_specs=specs,
        out_specs=jax.tree.map(lambda _: pl.BlockSpec(memory_space=pltpu.VMEM), out_shape),
        scratch_shapes=scratch,
    )(*args)


def swap_all(x, axes):
    return lax.all_to_all(x, axes, 0, 0, tiled=True)


def along_z(x, move, first=0):
    chips = range(first, CHIPS) if first >= 0 else range(-first)
    route = [(2 * z + c, 2 * ((z + move) % CHIPS) + c) for z in chips for c in range(2)]
    return lax.ppermute(x, SEQ, route)


def swap_pair(x):
    return lax.ppermute(x, "xp", [(0, 1), (1, 0)])


def scale_kernel(peaks_ref, dq_ref, dkv_ref, dx_ref, q_ref, kv_ref, x_ref):
    peaks = jnp.max(peaks_ref[...], axis=0, keepdims=True) + EPSILON
    q_ref[...] = (dq_ref[...] / peaks[:, 0:1]).astype(bf16)
    kv_ref[...] = (dkv_ref[...] / peaks[:, 1:2]).astype(bf16)
    x_ref[...] = (dx_ref[...] / peaks[:, 2:3]).astype(bf16)


def step(queries, key_value, grad_out, ssm_grad, b_proj, c_proj, decay_log, skip_gain):
    keys_here = lax.axis_index("xp") == 0
    pos = jnp.stack([lax.axis_index("z"), lax.axis_index("c")]).astype(jnp.int32)
    struct = jax.ShapeDtypeStruct

    other = swap_pair(key_value)
    shard = jnp.concatenate(
        [jnp.where(keys_here, key_value, other), jnp.where(keys_here, other, key_value)], axis=0
    )
    below = along_z(shard, 5)
    above = along_z(shard, -5)
    across = along_z(shard, 8, -8)
    three = jnp.concatenate([below, shard, above], axis=0)
    near = []
    for d in NEAR:
        near.append(along_z(three, -d) if d else three)

    state = call(state_kernel, struct((2 * CHIPS, 24, 128), bf16), ssm_grad, c_proj, decay_log)
    states = swap_all(state, SEQ)
    flows = call(scan_kernel, struct((2 * CHIPS, 16, 128), bf16), states)
    flow = swap_all(flows, SEQ)

    pieces = []
    for piece in near + [across]:
        pieces.append(lax.all_gather(piece, "c", axis=0, tiled=True).reshape(-1, TOK, 128))
    dq, dkv, peak_q = call(
        attention_kernel,
        (struct((TOK, 512), f32), struct((4 * CHIPS, TOK, 128), bf16), struct((8, 128), f32)),
        pos,
        queries,
        grad_out,
        *pieces,
        scratch=(
            pltpu.VMEM((4 * CHIPS, TOK, 128), bf16),
            pltpu.VMEM((256 * CHIPS, 512), f32),
            pltpu.VMEM((256 * CHIPS, 512), f32),
            pltpu.VMEM((128, 512), f32),
            pltpu.VMEM((128, 512), f32),
            pltpu.SemaphoreType.DMA((6,)),
        ),
        scalars=1,
        raw=6,
    )

    both = swap_all(dkv.reshape(2 * 4096, 128), "c").reshape(2, CHIPS, 2 * TOK, 128).astype(f32)
    chip_sum = (both[0] + both[1]).astype(bf16)
    parts = [chip_sum[6:9].astype(f32)]
    for k, d in enumerate(NEAR):
        if d:
            parts.append(along_z(chip_sum[3 * k : 3 * k + 3], d).astype(f32))
    three = (((parts[0] + parts[1]) + (parts[2] + parts[3])) + parts[4]).astype(bf16)
    from_above = along_z(three[0], -5)
    from_below = along_z(three[2], 5)
    from_across = along_z(chip_sum[15], -8, 8)
    own = (three[1].astype(f32) + from_across.astype(f32)) + (from_above.astype(f32) + from_below.astype(f32))
    mine = jnp.where(keys_here, own[:TOK], own[TOK:])
    other = jnp.where(keys_here, own[TOK:], own[:TOK]).astype(bf16)
    other = swap_pair(other)
    dx, peak_x = call(
        ssm_kernel,
        (struct((TOK, 512), f32), struct((8, 128), f32)),
        ssm_grad,
        b_proj,
        c_proj,
        decay_log,
        skip_gain.reshape(SSM_HEADS, 1),
        flow.reshape(512, 128),
    )

    dkv_own = mine + other.astype(f32)
    lane = lax.broadcasted_iota(jnp.int32, (1, 128), 1)
    early = jnp.where(lane == 0, peak_q[:1], peak_x[:1])
    early = lax.optimization_barrier(early)
    peaks = jnp.where(lane == 1, jnp.max(jnp.abs(dkv_own)), early)
    peaks = jnp.max(swap_all(jnp.tile(peaks, (32, 1)), SEQ), axis=0, keepdims=True)
    peaks = swap_all(jnp.tile(peaks, (16, 1)), HEAD)
    return call(
        scale_kernel,
        (struct((TOK, 512), bf16), struct((TOK, 128), bf16), struct((TOK, 512), bf16)),
        peaks,
        dq,
        dkv_own,
        dx,
    )


def solution(mesh):
    finer = Mesh(mesh.devices.reshape(SIZES), SEQ + HEAD)
    tokens = P(SEQ, HEAD)
    return jax.shard_map(
        step,
        mesh=finer,
        in_specs=(tokens, tokens, tokens, tokens, P(SEQ, None), P(SEQ, None), P(HEAD, SEQ), P(HEAD)),
        out_specs=(tokens, tokens, tokens),
        check_vma=False,
    )
```

```python
import math

import jax
import jax.numpy as jnp
from jax import lax
from jax.experimental import pallas as pl
from jax.experimental.pallas import tpu as pltpu
from jax.sharding import Mesh
from jax.sharding import PartitionSpec as P


SEQ = ("hi", "lo", "c")
HEAD = ("y", "xh", "xp")
SIZES = (4, 4, 2, 4, 2, 2)
NEAR = (-2, -1, 0, 1, 2)
CHIPS = 16
TOK = 128
SSM_HEADS = 8
SSM_DIM = 64
SCALE = 1.0 / math.sqrt(128)
EPSILON = 1e-6
HIGHEST = lax.Precision.HIGHEST
f32 = jnp.float32
bf16 = jnp.bfloat16


def dot(a, b, dims, precision=None):
    return lax.dot_general(a, b, (dims, ((), ())), precision=precision, preferred_element_type=f32)


NN = ((1,), (0,))
NT = ((1,), (1,))
TN = ((0,), (0,))


def heads_to_rows(x):
    return jnp.concatenate([x[:, 128 * h : 128 * (h + 1)] for h in range(4)], axis=0)


def attention_kernel(pos_ref, q_ref, do_ref, *refs):
    pieces, (dq_ref, dkv_ref, peak_ref, kv_ref, p_ref, dp_ref, outt_ref, dqt_ref, sems) = refs[:6], refs[6:]
    copies = []
    for k, piece in enumerate(pieces):
        count = piece.shape[0]
        copies.append(pltpu.make_async_copy(piece, kv_ref.at[pl.ds(12 * k, count)], sems.at[k]))
    for copy in copies:
        copy.start()
    chip, core = pos_ref[0], pos_ref[1]
    q = heads_to_rows(q_ref[...])
    do = heads_to_rows(do_ref[...])
    width = q.shape[0]

    steps = chip // 2 + 1

    def tiles(j):
        for z in (2 * j, 2 * j + 1):
            k = lax.rem(z - chip + 7 + CHIPS, CHIPS)
            near, far = lax.rem(k, 5), k // 5
            rel = lax.rem(lax.rem(z, 4) - lax.rem(chip, 4) + 4, 4)
            for c in range(2):
                held = jnp.where(k == 15, 60 + 2 * c, 12 * near + 6 * c + 2 * far)
                yield held, 2 * CHIPS * c + 8 * rel + 2 * (z // 4)

    def rows_at(j):
        return pl.ds(pl.multiple_of(j * 4 * TOK, 4 * TOK), 4 * TOK)

    def keys_at(j, part):
        return jnp.concatenate([kv_ref[held + part] for held, _ in tiles(j)], axis=0)

    def store_at(j, part, x):
        for k, (_, out) in enumerate(tiles(j)):
            dkv_ref[out + part] = x[TOK * k : TOK * (k + 1)]

    def partial_rows(x, op):
        return op(x.reshape(4 * TOK // 8, 8, width), axis=0)

    def score_step(j, carry, masked):
        old, total = carry
        s = dot(keys_at(j, 0), q, NT) * SCALE
        if masked:
            key = lax.broadcasted_iota(jnp.int32, s.shape, 0) + j * 4 * TOK
            query = lax.rem(lax.broadcasted_iota(jnp.int32, s.shape, 1), TOK) + (2 * chip + core) * TOK
            s = jnp.where(key <= query, s, -1e30)
        top = jnp.maximum(old, jnp.max(partial_rows(s, jnp.max), axis=0, keepdims=True))
        p_ref[rows_at(j), :] = s
        return top, total * jnp.exp(old - top) + partial_rows(jnp.exp(s - top), jnp.sum)

    for copy in copies:
        copy.wait()
    carry = score_step(steps - 1, (jnp.full((1, width), -1e30, f32), jnp.zeros((8, width), f32)), True)
    top, total = lax.fori_loop(0, steps - 1, lambda j, c: score_step(j, c, False), carry)
    lse = top + jnp.log(jnp.sum(total, axis=0, keepdims=True))
    outt_ref[...] = jnp.zeros_like(outt_ref)
    dqt_ref[...] = jnp.zeros_like(dqt_ref)

    def output_step(j, _):
        p = jnp.exp(p_ref[rows_at(j), :] - lse)
        p_ref[rows_at(j), :] = p
        p_b = p.astype(bf16)
        values = keys_at(j, 1)
        outt_ref[...] += dot(values, p_b, TN)
        dp_ref[rows_at(j), :] = dot(values, do, NT)
        store_at(j, 1, dot(p_b, do, NN).astype(bf16))
        return 0

    lax.fori_loop(0, steps, output_step, 0)
    dot_rows = jnp.concatenate([do_ref[:, 128 * h : 128 * (h + 1)].astype(f32).T for h in range(4)], axis=1)
    delta = jnp.sum(dot_rows * outt_ref[...].astype(bf16).astype(f32), axis=0, keepdims=True)

    def gradient_step(j, _):
        ds = (p_ref[rows_at(j), :] * (dp_ref[rows_at(j), :] - delta)).astype(bf16)
        store_at(j, 0, (dot(ds, q, NN) * SCALE).astype(bf16))
        dqt_ref[...] += dot(keys_at(j, 0), ds, TN)
        return 0

    lax.fori_loop(0, steps, gradient_step, 0)

    def clear_step(j, _):
        for part in range(2):
            store_at(j, part, jnp.zeros((4 * TOK, 128), bf16))
        return 0

    lax.fori_loop(steps, CHIPS // 2, clear_step, 0)
    dqt = dqt_ref[...] * SCALE
    for h in range(4):
        dq_ref[:, 128 * h : 128 * (h + 1)] = dqt[:, TOK * h : TOK * (h + 1)].T
    peak_ref[...] = jnp.broadcast_to(jnp.max(jnp.abs(dqt), keepdims=True), peak_ref.shape)


def spread_heads():
    shape = (SSM_HEADS, SSM_HEADS * SSM_DIM)
    row = lax.broadcasted_iota(jnp.int32, shape, 0)
    lane = lax.broadcasted_iota(jnp.int32, shape, 1)
    return (lane // SSM_DIM == row).astype(f32)


def running_decay(decay):
    row = lax.broadcasted_iota(jnp.int32, (TOK, TOK), 0)
    col = lax.broadcasted_iota(jnp.int32, (TOK, TOK), 1)
    lower = (col <= row).astype(f32)
    wide = dot(decay, spread_heads(), TN, HIGHEST)
    return dot(lower, wide, NN, HIGHEST)


def state_kernel(dy_ref, c_ref, decay_ref, out_ref):
    wide = running_decay(decay_ref[...])
    weighted = dy_ref[...].astype(f32) * jnp.exp(wide)
    states = dot(weighted.astype(bf16), c_ref[...], TN).astype(bf16)
    row = lax.broadcasted_iota(jnp.int32, (8, 128), 0)
    for k in range(2 * CHIPS):
        head = k * 16 // SSM_DIM
        total = jnp.broadcast_to(wide[TOK - 1 :, head * SSM_DIM : head * SSM_DIM + 1], (8, 128))
        high = total.astype(bf16).astype(f32)
        out_ref[k, :16, :] = states[16 * k : 16 * (k + 1), :]
        out_ref[k, 16:, :] = jnp.where(row == 0, high, total - high).astype(bf16)


def scan_kernel(state_ref, out_ref):
    flow = jnp.zeros((16, 128), f32)
    for k in reversed(range(2 * CHIPS)):
        out_ref[k] = flow.astype(bf16)
        total = state_ref[k, 16:, :].astype(f32)
        flow = state_ref[k, :16, :].astype(f32) + jnp.exp(total[:1] + total[1:2]) * flow


def ssm_kernel(dy_ref, b_ref, c_ref, decay_ref, skip_ref, flow_ref, dx_ref, peak_ref):
    decay = decay_ref[...]
    dy = dy_ref[...]
    wide = running_decay(decay)
    row = lax.broadcasted_iota(jnp.int32, (TOK, TOK), 0)
    col = lax.broadcasted_iota(jnp.int32, (TOK, TOK), 1)
    narrow = dot(decay, (row <= col).astype(f32), NN, HIGHEST)
    pairs = dot(b_ref[...], c_ref[...], NT)
    skip = jnp.sum(spread_heads() * skip_ref[...], axis=0, keepdims=True)
    carried = dot(b_ref[...], flow_ref[...], NT) * jnp.exp(wide[TOK - 1 :, :] - wide)
    rest = carried + skip * dy.astype(f32)
    top = jnp.zeros((1, 1), f32)
    for j in range(SSM_HEADS // 2):
        cols = slice(128 * j, 128 * (j + 1))
        both = dy[:, cols]
        out = rest[:, cols]
        for k in range(2):
            h = 2 * j + k
            span = narrow[h : h + 1, :] - wide[:, h * SSM_DIM : h * SSM_DIM + 1]
            weight = jnp.where(col >= row, jnp.exp(jnp.minimum(span, 0.0)), 0.0)
            kept = jnp.where(col // SSM_DIM == k, both, jnp.zeros_like(both))
            out = out + dot((pairs * weight).astype(bf16), kept, NN)
        dx_ref[:, cols] = out
        top = jnp.maximum(top, jnp.max(jnp.abs(out), keepdims=True))
    peak_ref[...] = jnp.broadcast_to(top, peak_ref.shape)


def call(body, out_shape, *args, scratch=(), scalars=0, raw=0):
    specs = [pl.BlockSpec(memory_space=pltpu.SMEM)] * scalars
    specs += [pl.BlockSpec(memory_space=pltpu.VMEM)] * (len(args) - scalars - raw)
    specs += [pl.BlockSpec(memory_space=pl.ANY)] * raw
    return pl.pallas_call(
        body,
        out_shape=out_shape,
        in_specs=specs,
        out_specs=jax.tree.map(lambda _: pl.BlockSpec(memory_space=pltpu.VMEM), out_shape),
        scratch_shapes=scratch,
    )(*args)


def swap_all(x, axes):
    return lax.all_to_all(x, axes, 0, 0, tiled=True)


def along_z(x, move, first=0):
    chips = range(first, CHIPS) if first >= 0 else range(-first)
    route = [(2 * z + c, 2 * ((z + move) % CHIPS) + c) for z in chips for c in range(2)]
    return lax.ppermute(x, SEQ, route)


def along_z_two(x):
    route = [(2 * z + c, 2 * ((z + 2 - 4 * c) % CHIPS) + c) for z in range(CHIPS) for c in range(2)]
    return lax.ppermute(x, SEQ, route)


def swap_pair(x):
    return lax.ppermute(x, "xp", [(0, 1), (1, 0)])


def scale_kernel(peaks_ref, dq_ref, dkv_ref, dx_ref, q_ref, kv_ref, x_ref):
    peaks = jnp.max(peaks_ref[...], axis=0, keepdims=True) + EPSILON
    q_ref[...] = (dq_ref[...] / peaks[:, 0:1]).astype(bf16)
    kv_ref[...] = (dkv_ref[...] / peaks[:, 1:2]).astype(bf16)
    x_ref[...] = (dx_ref[...] / peaks[:, 2:3]).astype(bf16)


def step(queries, key_value, grad_out, ssm_grad, b_proj, c_proj, decay_log, skip_gain):
    keys_here = lax.axis_index("xp") == 0
    pos = jnp.stack([lax.axis_index(("hi", "lo")), lax.axis_index("c")]).astype(jnp.int32)
    struct = jax.ShapeDtypeStruct

    other = swap_pair(key_value)
    shard = jnp.concatenate(
        [jnp.where(keys_here, key_value, other), jnp.where(keys_here, other, key_value)], axis=0
    )
    below = along_z(shard, 5)
    above = along_z(shard, -5)
    across = along_z(shard, 8, -8)
    three = jnp.concatenate([below, shard, above], axis=0)
    near = []
    for d in NEAR:
        near.append(along_z(three, -d) if d else three)

    state = call(state_kernel, struct((2 * CHIPS, 24, 128), bf16), ssm_grad, c_proj, decay_log)
    states = swap_all(state, SEQ)
    flows = call(scan_kernel, struct((2 * CHIPS, 16, 128), bf16), states)
    flow = swap_all(flows, SEQ)

    pieces = []
    for piece in near + [across]:
        pieces.append(lax.all_gather(piece, "c", axis=0, tiled=True).reshape(-1, TOK, 128))
    dq, dkv, peak_q = call(
        attention_kernel,
        (struct((TOK, 512), f32), struct((4 * CHIPS, TOK, 128), bf16), struct((8, 128), f32)),
        pos,
        queries,
        grad_out,
        *pieces,
        scratch=(
            pltpu.VMEM((4 * CHIPS, TOK, 128), bf16),
            pltpu.VMEM((256 * CHIPS, 512), f32),
            pltpu.VMEM((256 * CHIPS, 512), f32),
            pltpu.VMEM((128, 512), f32),
            pltpu.VMEM((128, 512), f32),
            pltpu.SemaphoreType.DMA((6,)),
        ),
        scalars=1,
        raw=6,
    )

    both = swap_all(dkv.reshape(2 * 4096, 128), "c").reshape(2, 4, 1024, 128).astype(f32)
    chip_sum = (both[0] + both[1]).astype(bf16)
    from_two = along_z_two(chip_sum[2])
    from_before = along_z(chip_sum[1], 1)
    from_after = along_z(chip_sum[3], -1)
    near = (
        (chip_sum[0].astype(f32) + from_before.astype(f32)) + (from_after.astype(f32) + from_two.astype(f32))
    ).astype(bf16)
    far = swap_all(near, ("hi", "xp")).reshape(8, TOK, 128)
    dx, peak_x = call(
        ssm_kernel,
        (struct((TOK, 512), f32), struct((8, 128), f32)),
        ssm_grad,
        b_proj,
        c_proj,
        decay_log,
        skip_gain.reshape(SSM_HEADS, 1),
        flow.reshape(512, 128),
    )

    dkv_own = jnp.sum(far.astype(f32), axis=0)
    lane = lax.broadcasted_iota(jnp.int32, (1, 128), 1)
    early = jnp.where(lane == 0, peak_q[:1], peak_x[:1])
    early = lax.optimization_barrier(early)
    peaks = jnp.where(lane == 1, jnp.max(jnp.abs(dkv_own)), early)
    peaks = jnp.max(swap_all(jnp.tile(peaks, (32, 1)), SEQ), axis=0, keepdims=True)
    peaks = swap_all(jnp.tile(peaks, (16, 1)), HEAD)
    return call(
        scale_kernel,
        (struct((TOK, 512), bf16), struct((TOK, 128), bf16), struct((TOK, 512), bf16)),
        peaks,
        dq,
        dkv_own,
        dx,
    )


def solution(mesh):
    finer = Mesh(mesh.devices.reshape(SIZES), SEQ + HEAD)
    tokens = P(SEQ, HEAD)
    return jax.shard_map(
        step,
        mesh=finer,
        in_specs=(tokens, tokens, tokens, tokens, P(SEQ, None), P(SEQ, None), P(HEAD, SEQ), P(HEAD)),
        out_specs=(tokens, tokens, tokens),
        check_vma=False,
    )
```

```python
import math

import jax
import jax.numpy as jnp
from jax import lax
from jax.experimental import pallas as pl
from jax.experimental.pallas import tpu as pltpu
from jax.sharding import Mesh
from jax.sharding import PartitionSpec as P


SEQ = ("hi", "lo", "c")
HEAD = ("y", "xh", "xp")
SIZES = (4, 4, 2, 4, 2, 2)
CHIPS = 16
TOK = 128
SSM_HEADS = 8
SSM_DIM = 64
SCALE = 1.0 / math.sqrt(128)
LOG2 = SCALE * math.log2(math.e)
EPSILON = 1e-6
HIGHEST = lax.Precision.HIGHEST
f32 = jnp.float32
bf16 = jnp.bfloat16


def dot(a, b, dims, precision=None):
    return lax.dot_general(a, b, (dims, ((), ())), precision=precision, preferred_element_type=f32)


NN = ((1,), (0,))
NT = ((1,), (1,))
TN = ((0,), (0,))


def heads_to_rows(x):
    return jnp.concatenate([x[:, 128 * h : 128 * (h + 1)] for h in range(4)], axis=0)


def attention_kernel(q_ref, do_ref, *refs):
    pieces, (dq_ref, dkv_ref, peak_ref, kv_ref, p_ref, dp_ref, top_ref, outt_ref, dqt_ref, sems) = refs[:4], refs[4:]
    copies = [pltpu.make_async_copy(piece, kv_ref.at[r], sems.at[r]) for r, piece in enumerate(pieces)]
    for copy in copies:
        copy.start()
    chip, core = lax.axis_index(("hi", "lo")), lax.axis_index("c")
    lane_group = lax.rem(chip, 4)
    q = heads_to_rows(q_ref[...])
    do = heads_to_rows(do_ref[...])
    width = q.shape[0]

    steps = chip // 2 + 1

    def place(z):
        return lax.rem(lax.rem(z, 4) - lane_group + 4, 4), z // 4

    def tiles(j):
        for z in (2 * j, 2 * j + 1):
            rel, hi = place(z)
            for c in range(2):
                yield rel, c, hi

    def rows_at(j):
        return pl.ds(pl.multiple_of(j * 4 * TOK, 4 * TOK), 4 * TOK)

    def keys_at(j, part):
        return jnp.concatenate([kv_ref[rel, c, 2 * hi + part] for rel, c, hi in tiles(j)], axis=0)

    def store_at(j, part, x):
        for k, (rel, c, hi) in enumerate(tiles(j)):
            dkv_ref[c, rel, hi, part] = x[TOK * k : TOK * (k + 1)]

    def partial_rows(x, op):
        return op(x.reshape(4 * TOK // 8, 8, width), axis=0)

    def score_step(j, carry, masked):
        old, total = carry
        s = dot(keys_at(j, 0), q, NT)
        dp_ref[rows_at(j), :] = dot(keys_at(j, 1), do, NT)
        if masked:
            key = lax.broadcasted_iota(jnp.int32, s.shape, 0) + j * 4 * TOK
            query = lax.rem(lax.broadcasted_iota(jnp.int32, s.shape, 1), TOK) + (2 * chip + core) * TOK
            s = jnp.where(key <= query, s, -1e30)
        top = jnp.maximum(old, jnp.max(partial_rows(s, jnp.max), axis=0, keepdims=True))
        e = jnp.exp2((s - top) * LOG2)
        p_ref[rows_at(j), :] = e
        top_ref[j] = jnp.broadcast_to(top, (8, width))
        return top, total * jnp.exp2((old - top) * LOG2) + partial_rows(e, jnp.sum)

    for copy in copies:
        copy.wait()
    carry = score_step(steps - 1, (jnp.full((1, width), -1e30, f32), jnp.zeros((8, width), f32)), True)
    top, total = lax.fori_loop(0, steps - 1, lambda j, c: score_step(j, c, False), carry)
    inverse = 1.0 / jnp.sum(total, axis=0, keepdims=True)
    outt_ref[...] = jnp.zeros_like(outt_ref)
    dqt_ref[...] = jnp.zeros_like(dqt_ref)

    def output_step(j, _):
        p = p_ref[rows_at(j), :] * (jnp.exp2((top_ref[j][:1] - top) * LOG2) * inverse)
        p_ref[rows_at(j), :] = p
        p_b = p.astype(bf16)
        outt_ref[...] += dot(keys_at(j, 1), p_b, TN)
        store_at(j, 1, dot(p_b, do, NN).astype(bf16))
        return 0

    lax.fori_loop(0, steps, output_step, 0)
    dot_rows = jnp.concatenate([do_ref[:, 128 * h : 128 * (h + 1)].astype(f32).T for h in range(4)], axis=1)
    delta = jnp.sum(dot_rows * outt_ref[...].astype(bf16).astype(f32), axis=0, keepdims=True)

    def gradient_step(j, _):
        ds = (p_ref[rows_at(j), :] * (dp_ref[rows_at(j), :] - delta)).astype(bf16)
        store_at(j, 0, (dot(ds, q, NN) * SCALE).astype(bf16))
        dqt_ref[...] += dot(keys_at(j, 0), ds, TN)
        return 0

    lax.fori_loop(0, steps, gradient_step, 0)

    def clear_step(j, _):
        for part in range(2):
            store_at(j, part, jnp.zeros((4 * TOK, 128), bf16))
        return 0

    lax.fori_loop(steps, CHIPS // 2, clear_step, 0)
    dqt = dqt_ref[...] * SCALE
    for h in range(4):
        dq_ref[:, 128 * h : 128 * (h + 1)] = dqt[:, TOK * h : TOK * (h + 1)].T
    peak_ref[...] = jnp.broadcast_to(jnp.max(jnp.abs(dqt), keepdims=True), peak_ref.shape)


def spread_heads():
    shape = (SSM_HEADS, SSM_HEADS * SSM_DIM)
    row = lax.broadcasted_iota(jnp.int32, shape, 0)
    lane = lax.broadcasted_iota(jnp.int32, shape, 1)
    return (lane // SSM_DIM == row).astype(f32)


def running_decay(decay):
    row = lax.broadcasted_iota(jnp.int32, (TOK, TOK), 0)
    col = lax.broadcasted_iota(jnp.int32, (TOK, TOK), 1)
    lower = (col <= row).astype(f32)
    wide = dot(decay, spread_heads(), TN, HIGHEST)
    return dot(lower, wide, NN, HIGHEST)


def state_kernel(dy_ref, c_ref, decay_ref, out_ref):
    wide = running_decay(decay_ref[...])
    weighted = dy_ref[...].astype(f32) * jnp.exp(wide)
    states = dot(weighted.astype(bf16), c_ref[...], TN).astype(bf16)
    row = lax.broadcasted_iota(jnp.int32, (8, 128), 0)
    for k in range(2 * CHIPS):
        head = k * 16 // SSM_DIM
        total = jnp.broadcast_to(wide[TOK - 1 :, head * SSM_DIM : head * SSM_DIM + 1], (8, 128))
        high = total.astype(bf16).astype(f32)
        out_ref[k, :16, :] = states[16 * k : 16 * (k + 1), :]
        out_ref[k, 16:, :] = jnp.where(row == 0, high, total - high).astype(bf16)


def scan_kernel(state_ref, out_ref):
    flow = jnp.zeros((16, 128), f32)
    for k in reversed(range(2 * CHIPS)):
        out_ref[k] = flow.astype(bf16)
        total = state_ref[k, 16:, :].astype(f32)
        flow = state_ref[k, :16, :].astype(f32) + jnp.exp(total[:1] + total[1:2]) * flow


def ssm_kernel(dy_ref, b_ref, c_ref, decay_ref, skip_ref, flow_ref, peak_q_ref, dx_ref, peak_ref):
    decay = decay_ref[...]
    dy = dy_ref[...]
    wide = running_decay(decay)
    row = lax.broadcasted_iota(jnp.int32, (TOK, TOK), 0)
    col = lax.broadcasted_iota(jnp.int32, (TOK, TOK), 1)
    narrow = dot(decay, (row <= col).astype(f32), NN, HIGHEST)
    pairs = dot(b_ref[...], c_ref[...], NT)
    skip = jnp.sum(spread_heads() * skip_ref[...], axis=0, keepdims=True)
    carried = dot(b_ref[...], flow_ref[...], NT) * jnp.exp(wide[TOK - 1 :, :] - wide)
    rest = carried + skip * dy.astype(f32)
    top = jnp.zeros((1, 1), f32)
    for j in range(SSM_HEADS // 2):
        cols = slice(128 * j, 128 * (j + 1))
        both = dy[:, cols]
        out = rest[:, cols]
        for k in range(2):
            h = 2 * j + k
            span = narrow[h : h + 1, :] - wide[:, h * SSM_DIM : h * SSM_DIM + 1]
            weight = jnp.where(col >= row, jnp.exp(jnp.minimum(span, 0.0)), 0.0)
            kept = jnp.where(col // SSM_DIM == k, both, jnp.zeros_like(both))
            out = out + dot((pairs * weight).astype(bf16), kept, NN)
        dx_ref[:, cols] = out
        top = jnp.maximum(top, jnp.max(jnp.abs(out), keepdims=True))
    lane = lax.broadcasted_iota(jnp.int32, peak_ref.shape, 1)
    peak_ref[...] = jnp.where(lane == 0, peak_q_ref[...], top)


def call(body, out_shape, *args, scratch=(), scalars=0, raw=0):
    specs = [pl.BlockSpec(memory_space=pltpu.SMEM)] * scalars
    specs += [pl.BlockSpec(memory_space=pltpu.VMEM)] * (len(args) - scalars - raw)
    specs += [pl.BlockSpec(memory_space=pl.ANY)] * raw
    return pl.pallas_call(
        body,
        out_shape=out_shape,
        in_specs=specs,
        out_specs=jax.tree.map(lambda _: pl.BlockSpec(memory_space=pltpu.VMEM), out_shape),
        scratch_shapes=scratch,
    )(*args)


def swap_all(x, axes):
    return lax.all_to_all(x, axes, 0, 0, tiled=True)


def along_z(x, step):
    route = []
    for chip in range(CHIPS):
        for core in range(2):
            move = step if step != 2 or core == 0 else -2
            route.append((2 * chip + core, 2 * ((chip + move) % CHIPS) + core))
    return lax.ppermute(x, SEQ, route)


def scale_kernel(peaks_ref, dq_ref, dkv_ref, dx_ref, q_ref, kv_ref, x_ref):
    peaks = jnp.max(peaks_ref[...], axis=0, keepdims=True) + EPSILON
    q_ref[...] = (dq_ref[...] / peaks[:, 0:1]).astype(bf16)
    kv_ref[...] = (dkv_ref[...] / peaks[:, 1:2]).astype(bf16)
    x_ref[...] = (dx_ref[...] / peaks[:, 2:3]).astype(bf16)


def step(queries, key_value, grad_out, ssm_grad, b_proj, c_proj, decay_log, skip_gain):
    struct = jax.ShapeDtypeStruct

    column = swap_all(jnp.tile(key_value, (8, 1)), ("hi", "xp"))
    two = along_z(column, 2)
    after = along_z(column, -1)
    before = along_z(column, 1)

    state = call(state_kernel, struct((2 * CHIPS, 24, 128), bf16), ssm_grad, c_proj, decay_log)
    states = swap_all(state, SEQ)
    flows = call(scan_kernel, struct((2 * CHIPS, 16, 128), bf16), states)
    flow = swap_all(flows, SEQ)

    pieces = []
    for piece in (column, after, two, before):
        pieces.append(lax.all_gather(piece, "c", axis=0, tiled=True).reshape(2, 8, TOK, 128))
    dq, dkv, peak_q = call(
        attention_kernel,
        (struct((TOK, 512), f32), struct((2, 4, 4, 2, TOK, 128), bf16), struct((8, 128), f32)),
        queries,
        grad_out,
        *pieces,
        scratch=(
            pltpu.VMEM((4, 2, 8, TOK, 128), bf16),
            pltpu.VMEM((256 * CHIPS, 512), f32),
            pltpu.VMEM((256 * CHIPS, 512), f32),
            pltpu.VMEM((CHIPS // 2, 8, 512), f32),
            pltpu.VMEM((128, 512), f32),
            pltpu.VMEM((128, 512), f32),
            pltpu.SemaphoreType.DMA((4,)),
        ),
        raw=4,
    )

    both = swap_all(dkv.reshape(2 * 4096, 128), "c").reshape(2, 4, 1024, 128).astype(f32)
    chip_sum = (both[0] + both[1]).astype(bf16)
    from_two = along_z(chip_sum[2], 2)
    from_before = along_z(chip_sum[1], 1)
    from_after = along_z(chip_sum[3], -1)
    near = (
        (chip_sum[0].astype(f32) + from_before.astype(f32)) + (from_after.astype(f32) + from_two.astype(f32))
    ).astype(bf16)
    far = swap_all(near, ("hi", "xp")).reshape(8, TOK, 128)
    dx, early = call(
        ssm_kernel,
        (struct((TOK, 512), f32), struct((8, 128), f32)),
        ssm_grad,
        b_proj,
        c_proj,
        decay_log,
        skip_gain.reshape(SSM_HEADS, 1),
        flow.reshape(512, 128),
        peak_q,
    )

    dkv_own = jnp.sum(far.astype(f32), axis=0)
    lane = lax.broadcasted_iota(jnp.int32, (1, 128), 1)
    peaks = jnp.where(lane == 1, jnp.max(jnp.abs(dkv_own)), early[:1])
    peaks = jnp.max(swap_all(jnp.tile(peaks, (32, 1)), SEQ), axis=0, keepdims=True)
    peaks = swap_all(jnp.tile(peaks, (16, 1)), HEAD)
    return call(
        scale_kernel,
        (struct((TOK, 512), bf16), struct((TOK, 128), bf16), struct((TOK, 512), bf16)),
        peaks,
        dq,
        dkv_own,
        dx,
    )


def solution(mesh):
    finer = Mesh(mesh.devices.reshape(SIZES), SEQ + HEAD)
    tokens = P(SEQ, HEAD)
    return jax.shard_map(
        step,
        mesh=finer,
        in_specs=(tokens, tokens, tokens, tokens, P(SEQ, None), P(SEQ, None), P(HEAD, SEQ), P(HEAD)),
        out_specs=(tokens, tokens, tokens),
        check_vma=False,
    )
```

```python
import math

import jax
import jax.numpy as jnp
from jax import lax
from jax.experimental import pallas as pl
from jax.experimental.pallas import tpu as pltpu
from jax.sharding import Mesh
from jax.sharding import PartitionSpec as P


SEQ = ("hi", "lo", "c")
HEAD = ("y", "xh", "xp")
SIZES = (4, 4, 2, 4, 2, 2)
CHIPS = 16
TOK = 128
SSM_HEADS = 8
SSM_DIM = 64
SCALE = 1.0 / math.sqrt(128)
LOG2 = SCALE * math.log2(math.e)
EPSILON = 1e-6
HIGHEST = lax.Precision.HIGHEST
f32 = jnp.float32
bf16 = jnp.bfloat16


def dot(a, b, dims, precision=None):
    return lax.dot_general(a, b, (dims, ((), ())), precision=precision, preferred_element_type=f32)


NN = ((1,), (0,))
NT = ((1,), (1,))
TN = ((0,), (0,))


def heads_to_rows(x):
    return jnp.concatenate([x[:, 128 * h : 128 * (h + 1)] for h in range(4)], axis=0)


def attention_kernel(q_ref, do_ref, *refs):
    pieces, (dq_ref, dkv_ref, peak_ref, kv_ref, p_ref, dp_ref, top_ref, outt_ref, dqt_ref, sems) = refs[:4], refs[4:]
    copies = [pltpu.make_async_copy(piece, kv_ref.at[r], sems.at[r]) for r, piece in enumerate(pieces)]
    for copy in copies:
        copy.start()
    chip, core = lax.axis_index(("hi", "lo")), lax.axis_index("c")
    lane_group = lax.rem(chip, 4)
    q = heads_to_rows(q_ref[...])
    do = heads_to_rows(do_ref[...])
    width = q.shape[0]

    pairs = chip // 4 + 1
    diagonal = chip // 2

    def place(z):
        return lax.rem(lax.rem(z, 4) - lane_group + 4, 4), z // 4

    def tiles(j):
        for z in (2 * j, 2 * j + 1):
            rel, hi = place(z)
            for c in range(2):
                yield rel, c, hi

    def rows_at(j):
        return pl.ds(pl.multiple_of(j * 4 * TOK, 4 * TOK), 4 * TOK)

    def keys_at(j, part):
        return jnp.concatenate([kv_ref[rel, c, 2 * hi + part] for rel, c, hi in tiles(j)], axis=0)

    def store_at(j, part, x):
        for k, (rel, c, hi) in enumerate(tiles(j)):
            dkv_ref[c, rel, hi, part] = x[TOK * k : TOK * (k + 1)]

    def partial_rows(x, op):
        return op(x.reshape(x.shape[0] // 8, 8, width), axis=0)

    def score_step(j, carry, masked):
        for half in range(2):
            carry = half_step(j, half, carry, masked)
        return carry

    def half_step(j, half, carry, masked):
        old, total = carry
        rows = pl.ds(pl.multiple_of(j * 4 * TOK, 4 * TOK) + 2 * half * TOK, 2 * TOK)
        held = list(tiles(j))[2 * half : 2 * half + 2]
        keys, values = (
            jnp.concatenate([kv_ref[rel, c, 2 * hi + part] for rel, c, hi in held], axis=0) for part in range(2)
        )
        s = dot(keys, q, NT)
        dp_ref[rows, :] = dot(values, do, NT)
        if masked:
            key = lax.broadcasted_iota(jnp.int32, s.shape, 0) + (j * 4 + 2 * half) * TOK
            query = lax.rem(lax.broadcasted_iota(jnp.int32, s.shape, 1), TOK) + (2 * chip + core) * TOK
            s = jnp.where(key <= query, s, -1e30)
        top = jnp.maximum(old, jnp.max(partial_rows(s, jnp.max), axis=0, keepdims=True))
        e = jnp.exp2((s - top) * LOG2)
        p_ref[rows, :] = e
        top_ref[2 * j + half] = jnp.broadcast_to(top, (8, width))
        return top, total * jnp.exp2((old - top) * LOG2) + partial_rows(e, jnp.sum)

    for copy in copies:
        copy.wait()
    carry = (jnp.full((1, width), -1e30, f32), jnp.zeros((8, width), f32))
    carry = lax.fori_loop(diagonal, 2 * pairs, lambda j, c: score_step(j, c, True), carry)
    carry = lax.cond(
        diagonal % 2 == 1, lambda c: score_step(diagonal - 1, c, False), lambda c: c, carry
    )
    top, total = lax.fori_loop(
        0, diagonal // 2, lambda i, c: score_step(2 * i + 1, score_step(2 * i, c, False), False), carry
    )
    inverse = 1.0 / jnp.sum(total, axis=0, keepdims=True)
    outt_ref[...] = jnp.zeros_like(outt_ref)
    dqt_ref[...] = jnp.zeros_like(dqt_ref)

    def output_step(i, _):
        step = jnp.zeros(outt_ref.shape, f32)
        for j in (2 * i, 2 * i + 1):
            scales = [jnp.exp2((top_ref[2 * j + half][:1] - top) * LOG2) * inverse for half in range(2)]
            p = p_ref[rows_at(j), :]
            p = jnp.concatenate([p[: 2 * TOK] * scales[0], p[2 * TOK :] * scales[1]], axis=0)
            p_ref[rows_at(j), :] = p
            p_b = p.astype(bf16)
            step = step + dot(keys_at(j, 1), p_b, TN)
            store_at(j, 1, dot(p_b, do, NN).astype(bf16))
        outt_ref[...] += step
        return 0

    lax.fori_loop(0, pairs, output_step, 0)
    dot_rows = jnp.concatenate([do_ref[:, 128 * h : 128 * (h + 1)].astype(f32).T for h in range(4)], axis=1)
    delta = jnp.sum(dot_rows * outt_ref[...].astype(bf16).astype(f32), axis=0, keepdims=True)

    def gradient_step(i, _):
        step = jnp.zeros(dqt_ref.shape, f32)
        for j in (2 * i, 2 * i + 1):
            ds = (p_ref[rows_at(j), :] * (dp_ref[rows_at(j), :] - delta)).astype(bf16)
            store_at(j, 0, (dot(ds, q, NN) * SCALE).astype(bf16))
            step = step + dot(keys_at(j, 0), ds, TN)
        dqt_ref[...] += step
        return 0

    lax.fori_loop(0, pairs, gradient_step, 0)

    def clear_step(j, _):
        for part in range(2):
            store_at(j, part, jnp.zeros((4 * TOK, 128), bf16))
        return 0

    lax.fori_loop(2 * pairs, CHIPS // 2, clear_step, 0)
    dqt = dqt_ref[...] * SCALE
    for h in range(4):
        dq_ref[:, 128 * h : 128 * (h + 1)] = dqt[:, TOK * h : TOK * (h + 1)].T
    peak_ref[...] = jnp.broadcast_to(jnp.max(jnp.abs(dqt), keepdims=True), peak_ref.shape)


def spread_heads():
    shape = (SSM_HEADS, SSM_HEADS * SSM_DIM)
    row = lax.broadcasted_iota(jnp.int32, shape, 0)
    lane = lax.broadcasted_iota(jnp.int32, shape, 1)
    return (lane // SSM_DIM == row).astype(f32)


def running_decay(decay):
    row = lax.broadcasted_iota(jnp.int32, (TOK, TOK), 0)
    col = lax.broadcasted_iota(jnp.int32, (TOK, TOK), 1)
    lower = (col <= row).astype(f32)
    wide = dot(decay, spread_heads(), TN, HIGHEST)
    return dot(lower, wide, NN, HIGHEST)


def state_kernel(dy_ref, c_ref, decay_ref, out_ref):
    wide = running_decay(decay_ref[...])
    weighted = dy_ref[...].astype(f32) * jnp.exp(wide)
    states = dot(weighted.astype(bf16), c_ref[...], TN).astype(bf16)
    row = lax.broadcasted_iota(jnp.int32, (8, 128), 0)
    for k in range(2 * CHIPS):
        head = k * 16 // SSM_DIM
        total = jnp.broadcast_to(wide[TOK - 1 :, head * SSM_DIM : head * SSM_DIM + 1], (8, 128))
        high = total.astype(bf16).astype(f32)
        out_ref[k, :16, :] = states[16 * k : 16 * (k + 1), :]
        out_ref[k, 16:, :] = jnp.where(row == 0, high, total - high).astype(bf16)


def scan_kernel(state_ref, out_ref):
    flow = jnp.zeros((16, 128), f32)
    for k in reversed(range(2 * CHIPS)):
        out_ref[k] = flow.astype(bf16)
        total = state_ref[k, 16:, :].astype(f32)
        flow = state_ref[k, :16, :].astype(f32) + jnp.exp(total[:1] + total[1:2]) * flow


def ssm_kernel(dy_ref, b_ref, c_ref, decay_ref, skip_ref, flow_ref, peak_q_ref, dx_ref, peak_ref):
    decay = decay_ref[...]
    dy = dy_ref[...]
    wide = running_decay(decay)
    row = lax.broadcasted_iota(jnp.int32, (TOK, TOK), 0)
    col = lax.broadcasted_iota(jnp.int32, (TOK, TOK), 1)
    narrow = dot(decay, (row <= col).astype(f32), NN, HIGHEST)
    pairs = dot(b_ref[...], c_ref[...], NT)
    skip = jnp.sum(spread_heads() * skip_ref[...], axis=0, keepdims=True)
    carried = dot(b_ref[...], flow_ref[...], NT) * jnp.exp(wide[TOK - 1 :, :] - wide)
    rest = carried + skip * dy.astype(f32)
    top = jnp.zeros((1, 1), f32)
    for j in range(SSM_HEADS // 2):
        cols = slice(128 * j, 128 * (j + 1))
        both = dy[:, cols]
        out = rest[:, cols]
        for k in range(2):
            h = 2 * j + k
            span = narrow[h : h + 1, :] - wide[:, h * SSM_DIM : h * SSM_DIM + 1]
            weight = jnp.where(col >= row, jnp.exp(jnp.minimum(span, 0.0)), 0.0)
            kept = jnp.where(col // SSM_DIM == k, both, jnp.zeros_like(both))
            out = out + dot((pairs * weight).astype(bf16), kept, NN)
        dx_ref[:, cols] = out
        top = jnp.maximum(top, jnp.max(jnp.abs(out), keepdims=True))
    lane = lax.broadcasted_iota(jnp.int32, peak_ref.shape, 1)
    peak_ref[...] = jnp.where(lane == 0, peak_q_ref[...], top)


def call(body, out_shape, *args, scratch=(), scalars=0, raw=0):
    specs = [pl.BlockSpec(memory_space=pltpu.SMEM)] * scalars
    specs += [pl.BlockSpec(memory_space=pltpu.VMEM)] * (len(args) - scalars - raw)
    specs += [pl.BlockSpec(memory_space=pl.ANY)] * raw
    return pl.pallas_call(
        body,
        out_shape=out_shape,
        in_specs=specs,
        out_specs=jax.tree.map(lambda _: pl.BlockSpec(memory_space=pltpu.VMEM), out_shape),
        scratch_shapes=scratch,
    )(*args)


def swap_all(x, axes):
    return lax.all_to_all(x, axes, 0, 0, tiled=True)


def along_z(x, step):
    route = []
    for chip in range(CHIPS):
        for core in range(2):
            move = step if step != 2 or core == 0 else -2
            route.append((2 * chip + core, 2 * ((chip + move) % CHIPS) + core))
    return lax.ppermute(x, SEQ, route)


def scale_kernel(peaks_ref, dq_ref, dkv_ref, dx_ref, q_ref, kv_ref, x_ref):
    peaks = jnp.max(peaks_ref[...], axis=0, keepdims=True) + EPSILON
    q_ref[...] = (dq_ref[...] / peaks[:, 0:1]).astype(bf16)
    kv_ref[...] = (dkv_ref[...] / peaks[:, 1:2]).astype(bf16)
    x_ref[...] = (dx_ref[...] / peaks[:, 2:3]).astype(bf16)


def step(queries, key_value, grad_out, ssm_grad, b_proj, c_proj, decay_log, skip_gain):
    struct = jax.ShapeDtypeStruct

    column = swap_all(jnp.tile(key_value, (8, 1)), ("hi", "xp"))
    two = along_z(column, 2)
    after = along_z(column, -1)
    before = along_z(column, 1)

    state = call(state_kernel, struct((2 * CHIPS, 24, 128), bf16), ssm_grad, c_proj, decay_log)
    states = swap_all(state, SEQ)
    flows = call(scan_kernel, struct((2 * CHIPS, 16, 128), bf16), states)
    flow = swap_all(flows, SEQ)

    pieces = []
    for piece in (column, after, two, before):
        pieces.append(lax.all_gather(piece, "c", axis=0, tiled=True).reshape(2, 8, TOK, 128))
    dq, dkv, peak_q = call(
        attention_kernel,
        (struct((TOK, 512), f32), struct((2, 4, 4, 2, TOK, 128), bf16), struct((8, 128), f32)),
        queries,
        grad_out,
        *pieces,
        scratch=(
            pltpu.VMEM((4, 2, 8, TOK, 128), bf16),
            pltpu.VMEM((256 * CHIPS, 512), f32),
            pltpu.VMEM((256 * CHIPS, 512), f32),
            pltpu.VMEM((CHIPS, 8, 512), f32),
            pltpu.VMEM((128, 512), f32),
            pltpu.VMEM((128, 512), f32),
            pltpu.SemaphoreType.DMA((4,)),
        ),
        raw=4,
    )

    both = swap_all(dkv.reshape(2 * 4096, 128), "c").reshape(2, 4, 1024, 128).astype(f32)
    chip_sum = (both[0] + both[1]).astype(bf16)
    from_two = along_z(chip_sum[2], 2)
    from_before = along_z(chip_sum[1], 1)
    from_after = along_z(chip_sum[3], -1)
    near = (
        (chip_sum[0].astype(f32) + from_before.astype(f32)) + (from_after.astype(f32) + from_two.astype(f32))
    ).astype(bf16)
    far = swap_all(near, ("hi", "xp")).reshape(8, TOK, 128)
    dx, early = call(
        ssm_kernel,
        (struct((TOK, 512), f32), struct((8, 128), f32)),
        ssm_grad,
        b_proj,
        c_proj,
        decay_log,
        skip_gain.reshape(SSM_HEADS, 1),
        flow.reshape(512, 128),
        peak_q,
    )

    dkv_own = jnp.sum(far.astype(f32), axis=0)
    lane = lax.broadcasted_iota(jnp.int32, (1, 128), 1)
    peaks = jnp.where(lane == 1, jnp.max(jnp.abs(dkv_own)), early[:1])
    peaks = jnp.max(swap_all(jnp.tile(peaks, (32, 1)), SEQ), axis=0, keepdims=True)
    peaks = swap_all(jnp.tile(peaks, (16, 1)), HEAD)
    return call(
        scale_kernel,
        (struct((TOK, 512), bf16), struct((TOK, 128), bf16), struct((TOK, 512), bf16)),
        peaks,
        dq,
        dkv_own,
        dx,
    )


def solution(mesh):
    finer = Mesh(mesh.devices.reshape(SIZES), SEQ + HEAD)
    tokens = P(SEQ, HEAD)
    return jax.shard_map(
        step,
        mesh=finer,
        in_specs=(tokens, tokens, tokens, tokens, P(SEQ, None), P(SEQ, None), P(HEAD, SEQ), P(HEAD)),
        out_specs=(tokens, tokens, tokens),
        check_vma=False,
    )
```

```python
import math

import jax
import jax.numpy as jnp
from jax import lax
from jax.experimental import pallas as pl
from jax.experimental.pallas import tpu as pltpu
from jax.sharding import Mesh
from jax.sharding import PartitionSpec as P


SEQ = ("hi", "lo", "c")
HEAD = ("y", "xh", "xp")
SIZES = (4, 4, 2, 4, 2, 2)
CHIPS = 16
TOK = 128
SSM_HEADS = 8
SSM_DIM = 64
SCALE = 1.0 / math.sqrt(128)
LOG2 = SCALE * math.log2(math.e)
EPSILON = 1e-6
HIGHEST = lax.Precision.HIGHEST
f32 = jnp.float32
bf16 = jnp.bfloat16


def dot(a, b, dims, precision=None):
    return lax.dot_general(a, b, (dims, ((), ())), precision=precision, preferred_element_type=f32)


NN = ((1,), (0,))
NT = ((1,), (1,))
TN = ((0,), (0,))


def heads_to_rows(x):
    return jnp.concatenate([x[:, 128 * h : 128 * (h + 1)] for h in range(4)], axis=0)


def attention_kernel(q_ref, do_ref, *refs):
    pieces, (dq_ref, dkv_ref, peak_ref, kv_ref, p_ref, dp_ref, top_ref, outt_ref, dqt_ref, sems) = refs[:4], refs[4:]
    copies = [pltpu.make_async_copy(piece, kv_ref.at[r], sems.at[r]) for r, piece in enumerate(pieces)]
    for copy in copies:
        copy.start()
    chip, core = lax.axis_index(("hi", "lo")), lax.axis_index("c")
    lane_group = lax.rem(chip, 4)
    q = heads_to_rows(q_ref[...])
    do = heads_to_rows(do_ref[...])
    width = q.shape[0]

    pairs = chip // 4 + 1
    diagonal = chip // 2

    def place(z):
        return lax.rem(lax.rem(z, 4) - lane_group + 4, 4), z // 4

    def tiles(j):
        for z in (2 * j, 2 * j + 1):
            rel, hi = place(z)
            for c in range(2):
                yield rel, c, hi

    def rows_at(j):
        return pl.ds(pl.multiple_of(j * 4 * TOK, 4 * TOK), 4 * TOK)

    def keys_at(j, part):
        return jnp.concatenate([kv_ref[rel, c, 2 * hi + part] for rel, c, hi in tiles(j)], axis=0)

    def store_at(j, part, x):
        for k, (rel, c, hi) in enumerate(tiles(j)):
            dkv_ref[c, rel, hi, part] = x[TOK * k : TOK * (k + 1)]

    def partial_rows(x, op):
        return op(x.reshape(x.shape[0] // 8, 8, width), axis=0)

    def score_step(j, carry, masked):
        for half in range(2):
            carry = half_step(j, half, carry, masked)
        return carry

    def half_step(j, half, carry, masked):
        old, total = carry
        rows = pl.ds(pl.multiple_of(j * 4 * TOK, 4 * TOK) + 2 * half * TOK, 2 * TOK)
        held = list(tiles(j))[2 * half : 2 * half + 2]
        keys, values = (
            jnp.concatenate([kv_ref[rel, c, 2 * hi + part] for rel, c, hi in held], axis=0) for part in range(2)
        )
        s = dot(keys, q, NT)
        dp_ref[rows, :] = dot(values, do, NT)
        if masked:
            key = lax.broadcasted_iota(jnp.int32, s.shape, 0) + (j * 4 + 2 * half) * TOK
            query = lax.rem(lax.broadcasted_iota(jnp.int32, s.shape, 1), TOK) + (2 * chip + core) * TOK
            s = jnp.where(key <= query, s, -1e30)
        top = jnp.maximum(old, jnp.max(partial_rows(s, jnp.max), axis=0, keepdims=True))
        e = jnp.exp2((s - top) * LOG2)
        p_ref[rows, :] = e
        top_ref[2 * j + half] = jnp.broadcast_to(top, (8, width))
        return top, total * jnp.exp2((old - top) * LOG2) + partial_rows(e, jnp.sum)

    for copy in copies:
        copy.wait()
    carry = (jnp.full((1, width), -1e30, f32), jnp.zeros((8, width), f32))
    carry = lax.fori_loop(diagonal, 2 * pairs, lambda j, c: score_step(j, c, True), carry)
    carry = lax.cond(
        diagonal % 2 == 1, lambda c: score_step(diagonal - 1, c, False), lambda c: c, carry
    )
    top, total = lax.fori_loop(
        0, diagonal // 2, lambda i, c: score_step(2 * i + 1, score_step(2 * i, c, False), False), carry
    )
    inverse = 1.0 / jnp.sum(total, axis=0, keepdims=True)
    outt_ref[...] = jnp.zeros_like(outt_ref)
    dqt_ref[...] = jnp.zeros_like(dqt_ref)

    def output_step(i, _):
        step = jnp.zeros(outt_ref.shape, f32)
        for j in (2 * i, 2 * i + 1):
            scales = [jnp.exp2((top_ref[2 * j + half][:1] - top) * LOG2) * inverse for half in range(2)]
            p = p_ref[rows_at(j), :]
            p = jnp.concatenate([p[: 2 * TOK] * scales[0], p[2 * TOK :] * scales[1]], axis=0)
            p_ref[rows_at(j), :] = p
            p_b = p.astype(bf16)
            step = step + dot(keys_at(j, 1), p_b, TN)
            store_at(j, 1, dot(p_b, do, NN).astype(bf16))
        outt_ref[...] += step
        return 0

    lax.fori_loop(0, pairs, output_step, 0)
    dot_rows = jnp.concatenate([do_ref[:, 128 * h : 128 * (h + 1)].astype(f32).T for h in range(4)], axis=1)
    delta = jnp.sum(dot_rows * outt_ref[...].astype(bf16).astype(f32), axis=0, keepdims=True)

    def gradient_step(i, _):
        step = jnp.zeros(dqt_ref.shape, f32)
        for j in (2 * i, 2 * i + 1):
            ds = (p_ref[rows_at(j), :] * (dp_ref[rows_at(j), :] - delta)).astype(bf16)
            store_at(j, 0, (dot(ds, q, NN) * SCALE).astype(bf16))
            step = step + dot(keys_at(j, 0), ds, TN)
        dqt_ref[...] += step
        return 0

    lax.fori_loop(0, pairs, gradient_step, 0)

    def clear_step(j, _):
        for part in range(2):
            store_at(j, part, jnp.zeros((4 * TOK, 128), bf16))
        return 0

    lax.fori_loop(2 * pairs, CHIPS // 2, clear_step, 0)
    dqt = dqt_ref[...] * SCALE
    for h in range(4):
        dq_ref[:, 128 * h : 128 * (h + 1)] = dqt[:, TOK * h : TOK * (h + 1)].T
    peak_ref[...] = jnp.broadcast_to(jnp.max(jnp.abs(dqt), keepdims=True), peak_ref.shape)


def spread_heads():
    shape = (SSM_HEADS, SSM_HEADS * SSM_DIM)
    row = lax.broadcasted_iota(jnp.int32, shape, 0)
    lane = lax.broadcasted_iota(jnp.int32, shape, 1)
    return (lane // SSM_DIM == row).astype(f32)


def running_decay(decay):
    row = lax.broadcasted_iota(jnp.int32, (TOK, TOK), 0)
    col = lax.broadcasted_iota(jnp.int32, (TOK, TOK), 1)
    lower = (col <= row).astype(f32)
    wide = dot(decay, spread_heads(), TN, HIGHEST)
    return dot(lower, wide, NN, HIGHEST)


def state_kernel(dy_ref, c_ref, decay_ref, out_ref):
    wide = running_decay(decay_ref[...])
    weighted = dy_ref[...].astype(f32) * jnp.exp(wide)
    states = dot(weighted.astype(bf16), c_ref[...], TN).astype(bf16)
    row = lax.broadcasted_iota(jnp.int32, (8, 128), 0)
    for k in range(2 * CHIPS):
        head = k * 16 // SSM_DIM
        total = jnp.broadcast_to(wide[TOK - 1 :, head * SSM_DIM : head * SSM_DIM + 1], (8, 128))
        high = total.astype(bf16).astype(f32)
        out_ref[k, :16, :] = states[16 * k : 16 * (k + 1), :]
        out_ref[k, 16:, :] = jnp.where(row == 0, high, total - high).astype(bf16)


def scan_kernel(state_ref, out_ref):
    flow = jnp.zeros((16, 128), f32)
    for k in reversed(range(2 * CHIPS)):
        out_ref[k] = flow.astype(bf16)
        total = state_ref[k, 16:, :].astype(f32)
        flow = state_ref[k, :16, :].astype(f32) + jnp.exp(total[:1] + total[1:2]) * flow


def ssm_kernel(dy_ref, b_ref, c_ref, decay_ref, skip_ref, flow_ref, peak_q_ref, dx_ref, peak_ref):
    decay = decay_ref[...]
    dy = dy_ref[...]
    wide = running_decay(decay)
    row = lax.broadcasted_iota(jnp.int32, (TOK, TOK), 0)
    col = lax.broadcasted_iota(jnp.int32, (TOK, TOK), 1)
    narrow = dot(decay, (row <= col).astype(f32), NN, HIGHEST)
    pairs = dot(b_ref[...], c_ref[...], NT)
    skip = jnp.sum(spread_heads() * skip_ref[...], axis=0, keepdims=True)
    carried = dot(b_ref[...], flow_ref[...], NT) * jnp.exp(wide[TOK - 1 :, :] - wide)
    rest = carried + skip * dy.astype(f32)
    top = jnp.zeros((1, 1), f32)
    for j in range(SSM_HEADS // 2):
        cols = slice(128 * j, 128 * (j + 1))
        both = dy[:, cols]
        out = rest[:, cols]
        for k in range(2):
            h = 2 * j + k
            span = narrow[h : h + 1, :] - wide[:, h * SSM_DIM : h * SSM_DIM + 1]
            weight = jnp.where(col >= row, jnp.exp(jnp.minimum(span, 0.0)), 0.0)
            kept = jnp.where(col // SSM_DIM == k, both, jnp.zeros_like(both))
            out = out + dot((pairs * weight).astype(bf16), kept, NN)
        dx_ref[:, cols] = out
        top = jnp.maximum(top, jnp.max(jnp.abs(out), keepdims=True))
    lane = lax.broadcasted_iota(jnp.int32, peak_ref.shape, 1)
    peak_ref[...] = jnp.where(lane == 0, peak_q_ref[:1], top)


def call(body, out_shape, *args, scratch=(), scalars=0, raw=0):
    specs = [pl.BlockSpec(memory_space=pltpu.SMEM)] * scalars
    specs += [pl.BlockSpec(memory_space=pltpu.VMEM)] * (len(args) - scalars - raw)
    specs += [pl.BlockSpec(memory_space=pl.ANY)] * raw
    return pl.pallas_call(
        body,
        out_shape=out_shape,
        in_specs=specs,
        out_specs=jax.tree.map(lambda _: pl.BlockSpec(memory_space=pltpu.VMEM), out_shape),
        scratch_shapes=scratch,
    )(*args)


def swap_all(x, axes):
    return lax.all_to_all(x, axes, 0, 0, tiled=True)


def along_z(x, step):
    route = []
    for chip in range(CHIPS):
        for core in range(2):
            move = step if step != 2 or core == 0 else -2
            route.append((2 * chip + core, 2 * ((chip + move) % CHIPS) + core))
    return lax.ppermute(x, SEQ, route)


def scale_kernel(peaks_ref, dq_ref, dkv_ref, dx_ref, q_ref, kv_ref, x_ref):
    peaks = jnp.max(peaks_ref[...], axis=0, keepdims=True) + EPSILON
    q_ref[...] = (dq_ref[...] / peaks[:, 0:1]).astype(bf16)
    kv_ref[...] = (dkv_ref[...] / peaks[:, 1:2]).astype(bf16)
    x_ref[...] = (dx_ref[...] / peaks[:, 2:3]).astype(bf16)


def step(queries, key_value, grad_out, ssm_grad, b_proj, c_proj, decay_log, skip_gain):
    struct = jax.ShapeDtypeStruct

    column = swap_all(jnp.tile(key_value, (8, 1)), ("hi", "xp"))
    two = along_z(column, 2)
    after = along_z(column, -1)
    before = along_z(column, 1)

    state = call(state_kernel, struct((2 * CHIPS, 24, 128), bf16), ssm_grad, c_proj, decay_log)
    states = swap_all(state, SEQ)
    flows = call(scan_kernel, struct((2 * CHIPS, 16, 128), bf16), states)
    flow = swap_all(flows, SEQ)

    pieces = []
    for piece in (column, after, two, before):
        pieces.append(lax.all_gather(piece, "c", axis=0, tiled=True).reshape(2, 8, TOK, 128))
    dq, dkv, peak_q = call(
        attention_kernel,
        (struct((TOK, 512), f32), struct((2, 4, 4, 2, TOK, 128), bf16), struct((8, 128), f32)),
        queries,
        grad_out,
        *pieces,
        scratch=(
            pltpu.VMEM((4, 2, 8, TOK, 128), bf16),
            pltpu.VMEM((256 * CHIPS, 512), f32),
            pltpu.VMEM((256 * CHIPS, 512), f32),
            pltpu.VMEM((CHIPS, 8, 512), f32),
            pltpu.VMEM((128, 512), f32),
            pltpu.VMEM((128, 512), f32),
            pltpu.SemaphoreType.DMA((4,)),
        ),
        raw=4,
    )

    both = swap_all(dkv.reshape(2 * 4096, 128), "c").reshape(2, 4, 1024, 128).astype(f32)
    chip_sum = (both[0] + both[1]).astype(bf16)
    from_two = along_z(chip_sum[2], 2)
    from_before = along_z(chip_sum[1], 1)
    from_after = along_z(chip_sum[3], -1)
    near = (
        (chip_sum[0].astype(f32) + from_before.astype(f32)) + (from_after.astype(f32) + from_two.astype(f32))
    ).astype(bf16)
    far = swap_all(near, ("hi", "xp")).reshape(8, TOK, 128)
    dx, early = call(
        ssm_kernel,
        (struct((TOK, 512), f32), struct((1, 128), f32)),
        ssm_grad,
        b_proj,
        c_proj,
        decay_log,
        skip_gain.reshape(SSM_HEADS, 1),
        flow.reshape(512, 128),
        peak_q,
    )

    dkv_own = jnp.sum(far.astype(f32), axis=0)
    lane = lax.broadcasted_iota(jnp.int32, (1, 128), 1)
    peaks = jnp.where(lane == 1, jnp.max(jnp.abs(dkv_own)), early)
    peaks = jnp.max(swap_all(jnp.tile(peaks, (32, 1)), SEQ), axis=0, keepdims=True)
    peaks = swap_all(jnp.tile(peaks, (16, 1)), HEAD)
    return call(
        scale_kernel,
        (struct((TOK, 512), bf16), struct((TOK, 128), bf16), struct((TOK, 512), bf16)),
        peaks,
        dq,
        dkv_own,
        dx,
    )


def solution(mesh):
    finer = Mesh(mesh.devices.reshape(SIZES), SEQ + HEAD)
    tokens = P(SEQ, HEAD)
    return jax.shard_map(
        step,
        mesh=finer,
        in_specs=(tokens, tokens, tokens, tokens, P(SEQ, None), P(SEQ, None), P(HEAD, SEQ), P(HEAD)),
        out_specs=(tokens, tokens, tokens),
        check_vma=False,
    )
```

```python
import math

import jax
import jax.numpy as jnp
from jax import lax
from jax.experimental import pallas as pl
from jax.experimental.pallas import tpu as pltpu
from jax.sharding import Mesh
from jax.sharding import PartitionSpec as P


SEQ = ("hi", "lo", "c")
HEAD = ("y", "xh", "xp")
SIZES = (4, 4, 2, 4, 2, 2)
CHIPS = 16
TOK = 128
SSM_HEADS = 8
SSM_DIM = 64
SCALE = 1.0 / math.sqrt(128)
LOG2 = SCALE * math.log2(math.e)
EPSILON = 1e-6
HIGHEST = lax.Precision.HIGHEST
f32 = jnp.float32
bf16 = jnp.bfloat16


def dot(a, b, dims, precision=None):
    return lax.dot_general(a, b, (dims, ((), ())), precision=precision, preferred_element_type=f32)


NN = ((1,), (0,))
NT = ((1,), (1,))
TN = ((0,), (0,))


def heads_to_rows(x):
    return jnp.concatenate([x[:, 128 * h : 128 * (h + 1)] for h in range(4)], axis=0)


def attention_kernel(q_ref, do_ref, *refs):
    pieces, (dq_ref, dkv_ref, peak_ref, kv_ref, p_ref, dp_ref, top_ref, outt_ref, dqt_ref, sems) = refs[:4], refs[4:]
    copies = [pltpu.make_async_copy(piece, kv_ref.at[r], sems.at[r]) for r, piece in enumerate(pieces)]
    for copy in copies:
        copy.start()
    chip, core = lax.axis_index(("hi", "lo")), lax.axis_index("c")
    lane_group = lax.rem(chip, 4)
    q = heads_to_rows(q_ref[...])
    do = heads_to_rows(do_ref[...])
    width = q.shape[0]

    diagonal = chip // 2
    pairs = (diagonal + 1) // 2

    def place(z):
        return lax.rem(lax.rem(z, 4) - lane_group + 4, 4), z // 4

    def tiles(j):
        for z in (2 * j, 2 * j + 1):
            rel, hi = place(z)
            for c in range(2):
                yield rel, c, hi

    def rows_at(j):
        return pl.ds(pl.multiple_of(j * 4 * TOK, 4 * TOK), 4 * TOK)

    def keys_at(j, part):
        return jnp.concatenate([kv_ref[rel, c, 2 * hi + part] for rel, c, hi in tiles(j)], axis=0)

    def store_at(j, part, x):
        for k, (rel, c, hi) in enumerate(tiles(j)):
            dkv_ref[c, rel, hi, part] = x[TOK * k : TOK * (k + 1)]

    def partial_rows(x, op):
        return op(x.reshape(x.shape[0] // 8, 8, width), axis=0)

    def score_step(j, carry, masked):
        for half in range(2):
            carry = half_step(j, half, carry, masked)
        return carry

    def half_step(j, half, carry, masked):
        old, total = carry
        rows = pl.ds(pl.multiple_of(j * 4 * TOK, 4 * TOK) + 2 * half * TOK, 2 * TOK)
        held = list(tiles(j))[2 * half : 2 * half + 2]
        keys, values = (
            jnp.concatenate([kv_ref[rel, c, 2 * hi + part] for rel, c, hi in held], axis=0) for part in range(2)
        )
        s = dot(keys, q, NT)
        dp_ref[rows, :] = dot(values, do, NT)
        if masked:
            key = lax.broadcasted_iota(jnp.int32, s.shape, 0) + (j * 4 + 2 * half) * TOK
            query = lax.rem(lax.broadcasted_iota(jnp.int32, s.shape, 1), TOK) + (2 * chip + core) * TOK
            s = jnp.where(key <= query, s, -1e30)
        top = jnp.maximum(old, jnp.max(partial_rows(s, jnp.max), axis=0, keepdims=True))
        e = jnp.exp2((s - top) * LOG2)
        p_ref[rows, :] = e
        top_ref[2 * j + half] = jnp.broadcast_to(top, (8, width))
        return top, total * jnp.exp2((old - top) * LOG2) + partial_rows(e, jnp.sum)

    for copy in copies:
        copy.wait()
    carry = (jnp.full((1, width), -1e30, f32), jnp.zeros((8, width), f32))
    carry = score_step(diagonal, carry, True)
    carry = lax.cond(
        diagonal % 2 == 1, lambda c: score_step(diagonal - 1, c, False), lambda c: c, carry
    )
    top, total = lax.fori_loop(
        0, diagonal // 2, lambda i, c: score_step(2 * i + 1, score_step(2 * i, c, False), False), carry
    )
    inverse = 1.0 / jnp.sum(total, axis=0, keepdims=True)
    outt_ref[...] = jnp.zeros_like(outt_ref)
    dqt_ref[...] = jnp.zeros_like(dqt_ref)

    def in_pairs(body):
        lax.fori_loop(0, pairs, lambda i, _: body((2 * i, 2 * i + 1)), 0)

        @pl.when(diagonal % 2 == 0)
        def _():
            body((diagonal,))

    def output_step(blocks):
        step = jnp.zeros(outt_ref.shape, f32)
        for j in blocks:
            scales = [jnp.exp2((top_ref[2 * j + half][:1] - top) * LOG2) * inverse for half in range(2)]
            p = p_ref[rows_at(j), :]
            p = jnp.concatenate([p[: 2 * TOK] * scales[0], p[2 * TOK :] * scales[1]], axis=0)
            p_ref[rows_at(j), :] = p
            p_b = p.astype(bf16)
            step = step + dot(keys_at(j, 1), p_b, TN)
            store_at(j, 1, dot(p_b, do, NN).astype(bf16))
        outt_ref[...] += step
        return 0

    in_pairs(output_step)
    dot_rows = jnp.concatenate([do_ref[:, 128 * h : 128 * (h + 1)].astype(f32).T for h in range(4)], axis=1)
    delta = jnp.sum(dot_rows * outt_ref[...].astype(bf16).astype(f32), axis=0, keepdims=True)

    def gradient_step(blocks):
        step = jnp.zeros(dqt_ref.shape, f32)
        for j in blocks:
            ds = (p_ref[rows_at(j), :] * (dp_ref[rows_at(j), :] - delta)).astype(bf16)
            store_at(j, 0, (dot(ds, q, NN) * SCALE).astype(bf16))
            step = step + dot(keys_at(j, 0), ds, TN)
        dqt_ref[...] += step
        return 0

    in_pairs(gradient_step)

    def clear_step(j, _):
        for part in range(2):
            store_at(j, part, jnp.zeros((4 * TOK, 128), bf16))
        return 0

    lax.fori_loop(diagonal + 1, CHIPS // 2, clear_step, 0)
    dqt = dqt_ref[...] * SCALE
    for h in range(4):
        dq_ref[:, 128 * h : 128 * (h + 1)] = dqt[:, TOK * h : TOK * (h + 1)].T
    peak_ref[...] = jnp.broadcast_to(jnp.max(jnp.abs(dqt), keepdims=True), peak_ref.shape)


def spread_heads():
    shape = (SSM_HEADS, SSM_HEADS * SSM_DIM)
    row = lax.broadcasted_iota(jnp.int32, shape, 0)
    lane = lax.broadcasted_iota(jnp.int32, shape, 1)
    return (lane // SSM_DIM == row).astype(f32)


def running_decay(decay):
    row = lax.broadcasted_iota(jnp.int32, (TOK, TOK), 0)
    col = lax.broadcasted_iota(jnp.int32, (TOK, TOK), 1)
    lower = (col <= row).astype(f32)
    wide = dot(decay, spread_heads(), TN, HIGHEST)
    return dot(lower, wide, NN, HIGHEST)


def state_kernel(dy_ref, c_ref, decay_ref, out_ref):
    wide = running_decay(decay_ref[...])
    weighted = dy_ref[...].astype(f32) * jnp.exp(wide)
    states = dot(weighted.astype(bf16), c_ref[...], TN).astype(bf16)
    row = lax.broadcasted_iota(jnp.int32, (8, 128), 0)
    for k in range(2 * CHIPS):
        head = k * 16 // SSM_DIM
        total = jnp.broadcast_to(wide[TOK - 1 :, head * SSM_DIM : head * SSM_DIM + 1], (8, 128))
        high = total.astype(bf16).astype(f32)
        out_ref[k, :16, :] = states[16 * k : 16 * (k + 1), :]
        out_ref[k, 16:, :] = jnp.where(row == 0, high, total - high).astype(bf16)


def scan_kernel(state_ref, out_ref):
    flow = jnp.zeros((16, 128), f32)
    for k in reversed(range(2 * CHIPS)):
        out_ref[k] = flow.astype(bf16)
        total = state_ref[k, 16:, :].astype(f32)
        flow = state_ref[k, :16, :].astype(f32) + jnp.exp(total[:1] + total[1:2]) * flow


def ssm_kernel(dy_ref, b_ref, c_ref, decay_ref, skip_ref, flow_ref, peak_q_ref, dx_ref, peak_ref):
    decay = decay_ref[...]
    dy = dy_ref[...]
    wide = running_decay(decay)
    row = lax.broadcasted_iota(jnp.int32, (TOK, TOK), 0)
    col = lax.broadcasted_iota(jnp.int32, (TOK, TOK), 1)
    narrow = dot(decay, (row <= col).astype(f32), NN, HIGHEST)
    pairs = dot(b_ref[...], c_ref[...], NT)
    skip = jnp.sum(spread_heads() * skip_ref[...], axis=0, keepdims=True)
    carried = dot(b_ref[...], flow_ref[...], NT) * jnp.exp(wide[TOK - 1 :, :] - wide)
    rest = carried + skip * dy.astype(f32)
    top = jnp.zeros((1, 1), f32)
    for j in range(SSM_HEADS // 2):
        cols = slice(128 * j, 128 * (j + 1))
        both = dy[:, cols]
        out = rest[:, cols]
        for k in range(2):
            h = 2 * j + k
            span = narrow[h : h + 1, :] - wide[:, h * SSM_DIM : h * SSM_DIM + 1]
            weight = jnp.where(col >= row, jnp.exp(jnp.minimum(span, 0.0)), 0.0)
            kept = jnp.where(col // SSM_DIM == k, both, jnp.zeros_like(both))
            out = out + dot((pairs * weight).astype(bf16), kept, NN)
        dx_ref[:, cols] = out
        top = jnp.maximum(top, jnp.max(jnp.abs(out), keepdims=True))
    lane = lax.broadcasted_iota(jnp.int32, peak_ref.shape, 1)
    peak_ref[...] = jnp.where(lane == 0, peak_q_ref[:1], top)


def call(body, out_shape, *args, scratch=(), scalars=0, raw=0):
    specs = [pl.BlockSpec(memory_space=pltpu.SMEM)] * scalars
    specs += [pl.BlockSpec(memory_space=pltpu.VMEM)] * (len(args) - scalars - raw)
    specs += [pl.BlockSpec(memory_space=pl.ANY)] * raw
    return pl.pallas_call(
        body,
        out_shape=out_shape,
        in_specs=specs,
        out_specs=jax.tree.map(lambda _: pl.BlockSpec(memory_space=pltpu.VMEM), out_shape),
        scratch_shapes=scratch,
    )(*args)


def swap_all(x, axes):
    return lax.all_to_all(x, axes, 0, 0, tiled=True)


def along_z(x, step):
    route = []
    for chip in range(CHIPS):
        for core in range(2):
            move = step if step != 2 or core == 0 else -2
            route.append((2 * chip + core, 2 * ((chip + move) % CHIPS) + core))
    return lax.ppermute(x, SEQ, route)


def scale_kernel(peaks_ref, dq_ref, dkv_ref, dx_ref, q_ref, kv_ref, x_ref):
    peaks = jnp.max(peaks_ref[...], axis=0, keepdims=True) + EPSILON
    q_ref[...] = (dq_ref[...] / peaks[:, 0:1]).astype(bf16)
    kv_ref[...] = (dkv_ref[...] / peaks[:, 1:2]).astype(bf16)
    x_ref[...] = (dx_ref[...] / peaks[:, 2:3]).astype(bf16)


def step(queries, key_value, grad_out, ssm_grad, b_proj, c_proj, decay_log, skip_gain):
    struct = jax.ShapeDtypeStruct

    column = swap_all(jnp.tile(key_value, (8, 1)), ("hi", "xp"))
    two = along_z(column, 2)
    after = along_z(column, -1)
    before = along_z(column, 1)

    state = call(state_kernel, struct((2 * CHIPS, 24, 128), bf16), ssm_grad, c_proj, decay_log)
    states = swap_all(state, SEQ)
    flows = call(scan_kernel, struct((2 * CHIPS, 16, 128), bf16), states)
    flow = swap_all(flows, SEQ)

    pieces = []
    for piece in (column, after, two, before):
        pieces.append(lax.all_gather(piece, "c", axis=0, tiled=True).reshape(2, 8, TOK, 128))
    dq, dkv, peak_q = call(
        attention_kernel,
        (struct((TOK, 512), f32), struct((2, 4, 4, 2, TOK, 128), bf16), struct((8, 128), f32)),
        queries,
        grad_out,
        *pieces,
        scratch=(
            pltpu.VMEM((4, 2, 8, TOK, 128), bf16),
            pltpu.VMEM((256 * CHIPS, 512), f32),
            pltpu.VMEM((256 * CHIPS, 512), f32),
            pltpu.VMEM((CHIPS, 8, 512), f32),
            pltpu.VMEM((128, 512), f32),
            pltpu.VMEM((128, 512), f32),
            pltpu.SemaphoreType.DMA((4,)),
        ),
        raw=4,
    )

    both = swap_all(dkv.reshape(2 * 4096, 128), "c").reshape(2, 4, 1024, 128).astype(f32)
    chip_sum = (both[0] + both[1]).astype(bf16)
    from_two = along_z(chip_sum[2], 2)
    from_before = along_z(chip_sum[1], 1)
    from_after = along_z(chip_sum[3], -1)
    near = (
        (chip_sum[0].astype(f32) + from_before.astype(f32)) + (from_after.astype(f32) + from_two.astype(f32))
    ).astype(bf16)
    far = swap_all(near, ("hi", "xp")).reshape(8, TOK, 128)
    dx, early = call(
        ssm_kernel,
        (struct((TOK, 512), f32), struct((1, 128), f32)),
        ssm_grad,
        b_proj,
        c_proj,
        decay_log,
        skip_gain.reshape(SSM_HEADS, 1),
        flow.reshape(512, 128),
        peak_q,
    )

    dkv_own = jnp.sum(far.astype(f32), axis=0)
    lane = lax.broadcasted_iota(jnp.int32, (1, 128), 1)
    peaks = jnp.where(lane == 1, jnp.max(jnp.abs(dkv_own)), early)
    peaks = jnp.max(swap_all(jnp.tile(peaks, (32, 1)), SEQ), axis=0, keepdims=True)
    peaks = swap_all(jnp.tile(peaks, (16, 1)), HEAD)
    return call(
        scale_kernel,
        (struct((TOK, 512), bf16), struct((TOK, 128), bf16), struct((TOK, 512), bf16)),
        peaks,
        dq,
        dkv_own,
        dx,
    )


def solution(mesh):
    finer = Mesh(mesh.devices.reshape(SIZES), SEQ + HEAD)
    tokens = P(SEQ, HEAD)
    return jax.shard_map(
        step,
        mesh=finer,
        in_specs=(tokens, tokens, tokens, tokens, P(SEQ, None), P(SEQ, None), P(HEAD, SEQ), P(HEAD)),
        out_specs=(tokens, tokens, tokens),
        check_vma=False,
    )
```
